256 devices in a mesh: rep: 16 (over y, x), shard: 16 (over z, core).
Axes of the slice: x: 4, y: 4, z: 8, core: 2. Of those that a mesh axis runs over, the one named last changes fastest.
Arguments:
- grad_wide: float32 [16, 1, 384, 5376], P('rep', None, 'shard')
- grad_down: float32 [16, 1, 1536, 384], P('rep', None, None, 'shard')
- grad_embed: float32 [16, 1001, 384], P('rep', None, 'shard')
- mom_wide: float32 [1, 384, 5376], P(None, 'shard'), may hold values from -6 to 6
- mom_down: float32 [1, 1536, 384], P(None, None, 'shard'), may hold values from -6 to 6
- mom_embed: float32 [1001, 384], P(None, 'shard'), may hold values from -6 to 6
Outputs:
- new_mom_wide: float32 [1, 384, 5376], P(None, 'shard')
- new_mom_down: float32 [1, 1536, 384], P(None, None, 'shard')
- new_mom_embed: float32 [1001, 384], P(None, 'shard')
- upd_wide: bfloat16 [1, 384, 5376], P(None, 'shard')
- upd_down: bfloat16 [1, 1536, 384], P(None, None, 'shard')
- upd_embed: bfloat16 [1001, 384], P(None, 'shard')
The draws below stay inside these ranges and needn't reach their ends.
All inputs are finite; a program needn't handle non-finite values.
Results may differ from the reference program's by a relative error of at most 0.03.
Values may be sent and summed in bfloat16 or wider, within the bound.
A program may use at most 64 MiB of HBM per device.

```python
import math
import jax
import jax.numpy as jnp
from jax import lax

D = 384
MLP = 1536
ADA = 2304
CLASSES = 1001
BLOCKS = 1
NS_ITERS = 5
QKV = 1152
WIDE = 5376
N_REP = 16


def scaled_gradient(key, lead, row_total, column_total):
    key_base, key_rows, key_columns = jax.random.split(key, 3)
    base = jax.random.normal(key_base, lead + (row_total, column_total), jnp.float32)
    row_scale = jnp.exp(jax.random.uniform(key_rows, (row_total, 1), jnp.float32, jnp.log(0.3), jnp.log(3.0)))
    column_scale = jnp.exp(jax.random.uniform(key_columns, (1, column_total), jnp.float32, jnp.log(0.3), jnp.log(3.0)))
    return base * row_scale * column_scale


def draw_grad_wide(key, part):
    return scaled_gradient(jax.random.fold_in(key, 11), (N_REP, BLOCKS), D, WIDE)


def draw_grad_down(key, part):
    return scaled_gradient(jax.random.fold_in(key, 12), (N_REP, BLOCKS), MLP, D)


def draw_grad_embed(key, part):
    return scaled_gradient(jax.random.fold_in(key, 13), (N_REP,), CLASSES, D)


def levels(own_key, dims, cuts, low, largest):
    loudness = 1.0
    for position, parts in cuts:
        heights = jax.random.uniform(jax.random.fold_in(jax.random.fold_in(own_key, 6), position), (parts,), jnp.float32, low / len(cuts), largest / len(cuts))
        loudness = loudness * jnp.repeat(jnp.exp(heights), dims[position] // parts).reshape((-1,) + (1,) * (len(dims) - 1 - position))
    return loudness


def normal_values(stream_key, dims, spread, limit, shards=(), held_as=jnp.bfloat16):
    array = jax.random.normal(stream_key, dims, jnp.float32) * spread
    if len(shards) > 0:
        array = levels(stream_key, dims, shards, -0.22, 0.18) * array
    return jnp.clip(array, min=-limit, max=limit).astype(held_as)


def setup_inputs(seed: int = 0) -> dict:
    key_of = jax.random.split(jax.random.key(seed), 7)
    grad_wide = draw_grad_wide(jax.random.fold_in(key_of[6], 71), 0)
    grad_down = draw_grad_down(jax.random.fold_in(key_of[6], 71), 0)
    grad_embed = draw_grad_embed(jax.random.fold_in(key_of[6], 71), 0)
    mom_wide = normal_values(key_of[3], (BLOCKS, D, WIDE), 1.0, 6.0, ((1, 16),), jnp.float32)
    mom_down = normal_values(key_of[4], (BLOCKS, MLP, D), 1.0, 6.0, ((2, 16),), jnp.float32)
    mom_embed = normal_values(key_of[5], (CLASSES, D), 1.0, 6.0, ((1, 16),), jnp.float32)
    return {"grad_wide": grad_wide, "grad_down": grad_down, "grad_embed": grad_embed, "mom_wide": mom_wide, "mom_down": mom_down, "mom_embed": mom_embed}


COEF_A = 3.4445
COEF_B = -4.775
COEF_C = 2.0315
MOMENTUM = 0.95
EPSILON = 1e-07

def orthogonal_update(nesterov):
    norm_value = jnp.sqrt(jnp.sum(nesterov * nesterov)) + EPSILON
    iterate = (nesterov / norm_value).astype(jnp.bfloat16)
    for sweep in range(NS_ITERS):
        gram = jnp.dot(iterate, iterate.T, preferred_element_type=jnp.float32).astype(jnp.bfloat16)
        polynomial = (COEF_B * gram.astype(jnp.float32) + COEF_C * jnp.dot(gram, gram, preferred_element_type=jnp.float32)).astype(jnp.bfloat16)
        iterate = (COEF_A * iterate.astype(jnp.float32) + jnp.dot(polynomial, iterate, preferred_element_type=jnp.float32)).astype(jnp.bfloat16)
    factor = math.sqrt(max(D, nesterov.shape[1]))
    return (iterate.astype(jnp.float32) * factor).astype(jnp.bfloat16)

def reference(grad_wide, grad_down, grad_embed, mom_wide, mom_down, mom_embed):
    g_wide = lax.optimization_barrier(jnp.sum(grad_wide, axis=0))
    g_down = lax.optimization_barrier(jnp.sum(grad_down, axis=0))
    g_embed = lax.optimization_barrier(jnp.sum(grad_embed, axis=0))
    new_wide = MOMENTUM * mom_wide + g_wide
    new_down = MOMENTUM * mom_down + g_down
    new_embed = MOMENTUM * mom_embed + g_embed
    nest_wide = g_wide + MOMENTUM * new_wide
    nest_down = g_down + MOMENTUM * new_down
    nest_embed = g_embed + MOMENTUM * new_embed
    segments = [(0, QKV), (QKV, D), (QKV + D, MLP), (QKV + D + MLP, ADA)]
    wide_list = []
    down_list = []
    for block in range(BLOCKS):
        pieces = [orthogonal_update(nest_wide[block][:, offset:offset + width]) for offset, width in segments]
        wide_list.append(jnp.concatenate(pieces, axis=1))
        down_list.append(orthogonal_update(nest_down[block].T).T)
    upd_wide = jnp.stack(wide_list)
    upd_down = jnp.stack(down_list)
    upd_embed = orthogonal_update(nest_embed.T).T
    return (new_wide, new_down, new_embed, upd_wide, upd_down, upd_embed)
```

```python
import math

import jax
import jax.numpy as jnp
from jax import lax
from jax.experimental import pallas as pl
from jax.experimental.pallas import tpu as pltpu
from jax.sharding import PartitionSpec as P

D = 384
COEF_A = 3.4445
COEF_B = -4.775
COEF_C = 2.0315
MOMENTUM = 0.95
EPSILON = 1e-07
NS_ITERS = 5

REP = 16
SHARD = 16
CHIPS_Z = 8
ROWS = D // SHARD
LANES = 128
WIDE, DOWN, EMBED = 5376, 1536, 1001
TILES = 62
SLOT = 5
STARTS = (0, 3, 6, 9, 12, 16, 20, 54, 24, 29, 34, 38, 42, 46, 50, 58)
WIDTHS = (3, 3, 3, 3, 4, 4, 4, 4, 5, 5, 4, 4, 4, 4, 4, 4)
FACTORS = (1152, 1152, 1152, 384, 1536, 1536, 1536, 1001) + (2304,) * 4 + (1536,) * 3 + (1001,)
MESH = pl.DeviceIdType.MESH
BF16 = jnp.bfloat16
F32 = jnp.float32


def tile_of(wide, down, embed, tile):
    if tile < 42:
        return wide[:, tile * LANES : (tile + 1) * LANES]
    if tile < 54:
        return down[:, (tile - 42) * LANES : (tile - 41) * LANES]
    first = (tile - 54) * LANES
    if tile < 61:
        return embed[:, first : first + LANES]
    part = embed[:, first:EMBED]
    return jnp.concatenate([part, jnp.zeros((ROWS, first + LANES - EMBED), part.dtype)], axis=1)


def put_tile(wide, down, embed, tile, value):
    if tile < 42:
        wide[:, tile * LANES : (tile + 1) * LANES] = value
    elif tile < 54:
        down[:, (tile - 42) * LANES : (tile - 41) * LANES] = value
    else:
        first = (tile - 54) * LANES
        width = min(LANES, EMBED - first)
        embed[:, first : first + width] = value[:, :width]


def split(value):
    high = value.astype(BF16)
    return high, (value - high.astype(F32)).astype(BF16)


def dot(left, right):
    return jnp.dot(left, right, preferred_element_type=F32)


def kernel(
    gw, gd, ge, mw, md, me_,
    ow, od, oe, uw, ud, ue,
    vgw, vgd, vge, vmw, vmd, vme,
    send, recv, slots_m, x, gall, part, group, rows_a, full_a, upd,
    onw, ond, one, ouw, oud, oue,
    load_sem, store_sem, rs_s, rs_r, rse_s, rse_r, ga_s, ga_r, gae_s, gae_r,
    z_s, z_r, ze_s, ze_r, f_s, f_r, fe_s, fe_r, gr_s, gr_r, az_s, az_r, af_s, af_r,
    up_s, up_r, upe_s, upe_r,
):
    r = lax.axis_index("rep")
    s = lax.axis_index("shard")
    z = s // 2
    c = s % 2
    partner = z * 2 + (1 - c)
    five = r // 2 == 4

    loads = [
        pltpu.make_async_copy(a, b, load_sem.at[i])
        for i, (a, b) in enumerate(((gw, vgw), (gd, vgd), (ge, vge), (mw, vmw), (md, vmd), (me_, vme)))
    ]
    for load in loads:
        load.start()

    barrier = pltpu.get_barrier_semaphore()

    def greet(device):
        pl.semaphore_signal(barrier, inc=1, device_id=device, device_id_type=MESH)

    x[SLOT - 1] = jnp.zeros((D, LANES), BF16)
    for d in range(1, REP):
        greet(((r + d) % REP, s))
    for d in range(1, CHIPS_Z):
        greet((r, (z + d) % CHIPS_Z * 2 + c))
    greet((r, partner))

    for load in loads[:3]:
        load.wait()
    for k in range(REP):
        for t in range(SLOT):
            if t < WIDTHS[k]:
                send[k, t] = tile_of(vgw, vgd, vge, STARTS[k] + t).astype(BF16)
            else:
                send[k, t] = jnp.zeros((ROWS, LANES), BF16)

    pl.semaphore_wait(barrier, REP - 1 + CHIPS_Z - 1 + 1)

    def rcopy(src, dst, ss, rs, device):
        return pltpu.make_async_remote_copy(
            src_ref=src, dst_ref=dst, send_sem=ss, recv_sem=rs, device_id=device, device_id_type=MESH
        )

    def rs(d):
        to = (r + d) % REP
        return rcopy(send.at[to, 0:4], recv.at[d, 0:4], rs_s.at[d], rs_r.at[d], (to, s))

    def rse(d):
        to = (r + d) % REP
        return rcopy(send.at[to, 4], recv.at[d, 4], rse_s.at[d], rse_r.at[d], (to, s))

    for d in range(1, REP):
        rs(d).start()

        @pl.when((r + d) % REP // 2 == 4)
        def _():
            rse(d).start()

    for load in loads[3:]:
        load.wait()
    for k in range(REP):
        for t in range(SLOT):
            if t < WIDTHS[k]:
                slots_m[k, t] = tile_of(vmw, vmd, vme, STARTS[k] + t)
            else:
                slots_m[k, t] = jnp.zeros((ROWS, LANES), F32)

    for d in range(1, REP):
        rs(d).wait_recv()

    my_rows = pl.ds(pl.multiple_of(s * ROWS, 8), ROWS)

    def reduce_tile(t):
        total = send[r, t].astype(F32)
        for d in range(1, REP):
            total = total + recv[d, t].astype(F32)
        momentum = MOMENTUM * slots_m[r, t] + total
        gall[r, t] = total.astype(BF16)
        x[t, my_rows, :] = (total + MOMENTUM * momentum).astype(BF16)

    for t in range(4):
        reduce_tile(t)

    @pl.when(five)
    def _():
        for d in range(1, REP):
            rse(d).wait_recv()
        reduce_tile(4)

    def rows_of(shard):
        return pl.ds(pl.multiple_of(shard * ROWS, 8), ROWS)

    def z_from(d):
        return (z - d + CHIPS_Z) % CHIPS_Z * 2 + c

    def zc(d):
        ref = x.at[0:4, my_rows, :]
        return rcopy(ref, ref, z_s.at[d], z_r.at[d], (r, (z + d) % CHIPS_Z * 2 + c))

    def zce(d):
        ref = x.at[4, my_rows, :]
        return rcopy(ref, ref, ze_s.at[d], ze_r.at[d], (r, (z + d) % CHIPS_Z * 2 + c))

    def fc(d):
        ref = x.at[0:4, rows_of(z_from(d)), :]
        return rcopy(ref, ref, f_s.at[d], f_r.at[d], (r, partner))

    def fce(d):
        ref = x.at[4, rows_of(z_from(d)), :]
        return rcopy(ref, ref, fe_s.at[d], fe_r.at[d], (r, partner))

    near = (1, 7, 2, 6, 3, 5, 4)
    for d in near:
        zc(d).start()

        @pl.when(five)
        def _():
            zce(d).start()

    fc(0).start()

    @pl.when(five)
    def _():
        fce(0).start()

    def ga(d):
        ref = gall.at[r, 0:4]
        return rcopy(ref, ref, ga_s.at[d], ga_r.at[d], ((r + d) % REP, s))

    def gae(d):
        ref = gall.at[r, 4]
        return rcopy(ref, ref, gae_s.at[d], gae_r.at[d], ((r + d) % REP, s))

    for d in range(1, REP):
        ga(d).start()

        @pl.when(five)
        def _():
            gae(d).start()

    for d in near:
        zc(d).wait_recv()
        fc(d).start()

        @pl.when(five)
        def _():
            zce(d).wait_recv()
            fce(d).start()

    for d in range(CHIPS_Z):
        fc(d).wait_recv()

        @pl.when(five)
        def _():
            fce(d).wait_recv()

    def whole_x():
        return jnp.concatenate([x[t] for t in range(SLOT)], axis=1)

    mine = jnp.concatenate([x[t, my_rows, :] for t in range(SLOT)], axis=1)
    gram = lax.dot_general(mine, whole_x(), (((1,), (1,)), ((), ())), preferred_element_type=F32)
    for j in range(3):
        part[j] = gram[:, j * LANES : (j + 1) * LANES]

    first = jnp.where(r // 4 == 2, 8, r // 4 * 4)
    count = jnp.where(r // 4 == 2, 4, 3)
    embed = jnp.logical_or(r == 7, r == 15)
    count = jnp.where(embed, 2, jnp.where(r == 3, 1, count))

    def member(d):
        place = r - first + d
        inside = first + jnp.where(place >= count, place - count, place)
        return jnp.where(embed, (r + 8) % REP, inside)

    def gr(d):
        return rcopy(part, group.at[d], gr_s.at[d], gr_r.at[d], (member(d), s))

    for d in range(1, 4):

        @pl.when(d < count)
        def _():
            gr(d).start()

    rows_a[...] = part[...]
    for d in range(1, 4):

        @pl.when(d < count)
        def _():
            gr(d).wait_recv()
            rows_a[...] = rows_a[...] + group[d]

    full_a[:, my_rows, :] = rows_a[...]

    def az(d):
        ref = full_a.at[:, my_rows, :]
        return rcopy(ref, ref, az_s.at[d], az_r.at[d], (r, (z + d) % CHIPS_Z * 2 + c))

    def af(d):
        ref = full_a.at[:, rows_of(z_from(d)), :]
        return rcopy(ref, ref, af_s.at[d], af_r.at[d], (r, partner))

    for d in near:
        az(d).start()
    af(0).start()

    for d in range(1, REP):
        ga(d).wait_recv()

        @pl.when((r - d + REP) % REP // 2 == 4)
        def _():
            src = (r - d + REP) % REP
            ref = gall.at[src, 4]
            rcopy(ref, ref, gae_s.at[d], gae_r.at[d], (src, s)).wait_recv()

    for k in range(REP):
        for t in range(WIDTHS[k]):
            put_tile(onw, ond, one, STARTS[k] + t, MOMENTUM * slots_m[k, t] + gall[k, t].astype(F32))
    stores = [
        pltpu.make_async_copy(a, b, store_sem.at[i])
        for i, (a, b) in enumerate(((onw, ow), (ond, od), (one, oe), (ouw, uw), (oud, ud), (oue, ue)))
    ]
    for store in stores[:3]:
        store.start()

    for d in near:
        az(d).wait_recv()
        af(d).start()
    for d in range(CHIPS_Z):
        af(d).wait_recv()

    a = jnp.concatenate([full_a[j] for j in range(3)], axis=1)
    row = lax.broadcasted_iota(jnp.int32, (D, D), 0)
    column = lax.broadcasted_iota(jnp.int32, (D, D), 1)
    trace = jnp.sum(jnp.sum(jnp.where(row == column, a, 0.0), axis=1, keepdims=True), axis=0, keepdims=True)
    scale = 1.0 / (jnp.sqrt(trace) + EPSILON)
    a = a * scale * scale
    eye_rows = (
        lax.broadcasted_iota(jnp.int32, (ROWS, D), 0) + s * ROWS == lax.broadcasted_iota(jnp.int32, (ROWS, D), 1)
    ).astype(F32)
    q = eye_rows
    for step in range(NS_ITERS):
        ah, al = split(a)
        qh, ql = split(q)
        last = step == NS_ITERS - 1

        def times_a(uh, ul):
            both = dot(jnp.concatenate([uh, ul], axis=0), ah)
            n = uh.shape[0]
            return both[:n] + both[n:] + dot(uh, al)

        if last:
            qa = times_a(qh, ql)
            qa2 = times_a(*split(qa))
        else:
            a2 = times_a(ah, al)
            qa = times_a(qh, ql)
            a3 = times_a(*split(a2))
            qa2 = times_a(*split(qa))
            b = COEF_A * a + COEF_B * a2 + COEF_C * a3
            bh, bl = split(b)
            th, tl = split(COEF_B * a + COEF_C * a2)
            both = dot(jnp.concatenate([th, tl], axis=0), bh)
            a = COEF_A * b + both[:D] + both[D:] + dot(th, bl)
        q = COEF_A * q + COEF_B * qa + COEF_C * qa2

    factor = jnp.float32(0.0)
    for k in range(REP):
        factor = factor + jnp.where(r == k, jnp.float32(math.sqrt(max(D, FACTORS[k]))), jnp.float32(0.0))
    result = (dot(q.astype(BF16), whole_x()) * (scale * factor)).astype(BF16)
    for t in range(SLOT):
        upd[r, t] = result[:, t * LANES : (t + 1) * LANES]

    def up(d):
        ref = upd.at[r, 0:4]
        return rcopy(ref, ref, up_s.at[d], up_r.at[d], ((r + d) % REP, s))

    def upe(d):
        ref = upd.at[r, 4]
        return rcopy(ref, ref, upe_s.at[d], upe_r.at[d], ((r + d) % REP, s))

    for d in range(1, REP):
        up(d).start()

        @pl.when(five)
        def _():
            upe(d).start()

    for d in range(1, REP):
        rs(d).wait_send()
        ga(d).wait_send()

        @pl.when((r + d) % REP // 2 == 4)
        def _():
            rse(d).wait_send()

        @pl.when(five)
        def _():
            gae(d).wait_send()

    for d in range(CHIPS_Z):
        if d:
            zc(d).wait_send()
            az(d).wait_send()
        fc(d).wait_send()
        af(d).wait_send()

        @pl.when(five)
        def _():
            if d:
                zce(d).wait_send()
            fce(d).wait_send()

    for d in range(1, 4):

        @pl.when(d < count)
        def _():
            gr(d).wait_send()

    for d in range(1, REP):
        up(d).wait_recv()

        @pl.when((r - d + REP) % REP // 2 == 4)
        def _():
            src = (r - d + REP) % REP
            ref = upd.at[src, 4]
            rcopy(ref, ref, upe_s.at[d], upe_r.at[d], (src, s)).wait_recv()

    for k in range(REP):
        for t in range(WIDTHS[k]):
            put_tile(ouw, oud, oue, STARTS[k] + t, upd[k, t])
    for store in stores[3:]:
        store.start()
    for d in range(1, REP):
        up(d).wait_send()

        @pl.when(five)
        def _():
            upe(d).wait_send()

    for store in stores:
        store.wait()


def per_device(grad_wide, grad_down, grad_embed, mom_wide, mom_down, mom_embed):
    any_space = pl.BlockSpec(memory_space=pl.ANY)
    shapes = [(ROWS, WIDE), (ROWS, DOWN), (ROWS, EMBED)]
    dma = pltpu.SemaphoreType.DMA
    scratch = (
        [pltpu.VMEM(shape, F32) for shape in shapes] * 2
        + [
            pltpu.VMEM((REP, SLOT, ROWS, LANES), BF16),
            pltpu.VMEM((REP, SLOT, ROWS, LANES), BF16),
            pltpu.VMEM((REP, SLOT, ROWS, LANES), F32),
            pltpu.VMEM((SLOT, D, LANES), BF16),
            pltpu.VMEM((REP, SLOT, ROWS, LANES), BF16),
            pltpu.VMEM((3, ROWS, LANES), F32),
            pltpu.VMEM((4, 3, ROWS, LANES), F32),
            pltpu.VMEM((3, ROWS, LANES), F32),
            pltpu.VMEM((3, D, LANES), F32),
            pltpu.VMEM((REP, SLOT, ROWS, LANES), BF16),
        ]
        + [pltpu.VMEM(shape, F32) for shape in shapes]
        + [pltpu.VMEM(shape, BF16) for shape in shapes]
        + [dma((6,)), dma((6,))]
        + [dma((REP,))] * 8
        + [dma((CHIPS_Z,))] * 8
        + [dma((4,))] * 2
        + [dma((CHIPS_Z,))] * 4
        + [dma((REP,))] * 4
    )
    outs = pl.pallas_call(
        kernel,
        out_shape=[jax.ShapeDtypeStruct(shape, F32) for shape in shapes]
        + [jax.ShapeDtypeStruct(shape, BF16) for shape in shapes],
        in_specs=[any_space] * 6,
        out_specs=[any_space] * 6,
        scratch_shapes=scratch,
        compiler_params=pltpu.CompilerParams(
            collective_id=0, has_side_effects=True, vmem_limit_bytes=40 * 1024 * 1024
        ),
        name="muon",
    )(
        grad_wide[0, 0],
        grad_down[0, 0].T,
        grad_embed[0].T,
        mom_wide[0],
        mom_down[0].T,
        mom_embed.T,
    )
    new_wide, new_down, new_embed, upd_wide, upd_down, upd_embed = outs
    return (
        new_wide[None],
        new_down.T[None],
        new_embed.T,
        upd_wide[None],
        upd_down.T[None],
        upd_embed.T,
    )


def solution(mesh):
    return jax.shard_map(
        per_device,
        mesh=mesh,
        in_specs=(
            P("rep", None, "shard", None),
            P("rep", None, None, "shard"),
            P("rep", None, "shard"),
            P(None, "shard", None),
            P(None, None, "shard"),
            P(None, "shard"),
        ),
        out_specs=(
            P(None, "shard", None),
            P(None, None, "shard"),
            P(None, "shard"),
        )
        * 2,
        check_vma=False,
    )
```

```python
import math

import jax
import jax.numpy as jnp
from jax import lax
from jax.experimental import pallas as pl
from jax.experimental.pallas import tpu as pltpu
from jax.sharding import PartitionSpec as P

D = 384
COEF_A = 3.4445
COEF_B = -4.775
COEF_C = 2.0315
MOMENTUM = 0.95
EPSILON = 1e-07
NS_ITERS = 5

REP = 16
SHARD = 16
CHIPS_Z = 8
ROWS = D // SHARD
LANES = 128
WIDE, DOWN, EMBED = 5376, 1536, 1001
TILES = 62
SLOT = 5
GROUPS = 6
STARTS = (0, 3, 6, 9, 12, 16, 20, 54, 24, 29, 34, 38, 42, 46, 50, 58)
WIDTHS = (3, 3, 3, 3, 4, 4, 4, 4, 5, 5, 4, 4, 4, 4, 4, 4)
FACTORS = (1152, 1152, 1152, 384, 1536, 1536, 1536, 1001) + (2304,) * 4 + (1536,) * 3 + (1001,)
MESH = pl.DeviceIdType.MESH
BF16 = jnp.bfloat16
F32 = jnp.float32


def tile_of(wide, down, embed, tile):
    if tile < 42:
        return wide[:, tile * LANES : (tile + 1) * LANES]
    if tile < 54:
        return down[:, (tile - 42) * LANES : (tile - 41) * LANES]
    first = (tile - 54) * LANES
    if tile < 61:
        return embed[:, first : first + LANES]
    part = embed[:, first:EMBED]
    return jnp.concatenate([part, jnp.zeros((ROWS, first + LANES - EMBED), part.dtype)], axis=1)


def put_tile(wide, down, embed, tile, value):
    if tile < 42:
        wide[:, tile * LANES : (tile + 1) * LANES] = value
    elif tile < 54:
        down[:, (tile - 42) * LANES : (tile - 41) * LANES] = value
    else:
        first = (tile - 54) * LANES
        width = min(LANES, EMBED - first)
        embed[:, first : first + width] = value[:, :width]


def split(value):
    high = value.astype(BF16)
    return high, (value - high.astype(F32)).astype(BF16)


def dot(left, right):
    return jnp.dot(left, right, preferred_element_type=F32)


def kernel(
    gw, gd, ge, mw, md, me_,
    ow, od, oe, uw, ud, ue,
    vgw, vgd, vge, vmw, vmd, vme,
    send, recv, slots_m, x, gall, part, group, tri, upd,
    load_sem, rs_s, rs_r, rse_s, rse_r, ga_s, ga_r, gae_s, gae_r,
    z_s, z_r, ze_s, ze_r, f_s, f_r, fe_s, fe_r, gr_s, gr_r, az_s, az_r, af_s, af_r,
    up_s, up_r, upe_s, upe_r,
):
    r = lax.axis_index("rep")
    s = lax.axis_index("shard")
    z = s // 2
    c = s % 2
    partner = z * 2 + (1 - c)
    five = r // 2 == 4

    loads = [
        pltpu.make_async_copy(a, b, load_sem.at[i])
        for i, (a, b) in enumerate(((gw, vgw), (gd, vgd), (ge, vge), (mw, vmw), (md, vmd), (me_, vme)))
    ]
    for load in loads:
        load.start()

    barrier = pltpu.get_barrier_semaphore()

    def greet(device):
        pl.semaphore_signal(barrier, inc=1, device_id=device, device_id_type=MESH)

    x[SLOT - 1] = jnp.zeros((D, LANES), BF16)
    for d in range(1, REP):
        greet(((r + d) % REP, s))
    for d in range(1, CHIPS_Z):
        greet((r, (z + d) % CHIPS_Z * 2 + c))
    greet((r, partner))

    for load in loads[:3]:
        load.wait()
    for k in range(REP):
        for t in range(SLOT):
            if t < WIDTHS[k]:
                send[k, t] = tile_of(vgw, vgd, vge, STARTS[k] + t).astype(BF16)
            else:
                send[k, t] = jnp.zeros((ROWS, LANES), BF16)

    pl.semaphore_wait(barrier, REP - 1 + CHIPS_Z - 1 + 1)

    def rcopy(src, dst, ss, rs, device):
        return pltpu.make_async_remote_copy(
            src_ref=src, dst_ref=dst, send_sem=ss, recv_sem=rs, device_id=device, device_id_type=MESH
        )

    def tiles(chunk):
        return pl.ds(2 * chunk, 2)

    def rs(d, chunk):
        to = (r + d) % REP
        return rcopy(
            send.at[to, tiles(chunk)], recv.at[d, tiles(chunk)], rs_s.at[chunk, d], rs_r.at[chunk, d], (to, s)
        )

    def rse(d):
        to = (r + d) % REP
        return rcopy(send.at[to, 4], recv.at[d, 4], rse_s.at[d], rse_r.at[d], (to, s))

    for chunk in range(2):
        for d in range(1, REP):
            rs(d, chunk).start()

    for d in range(1, REP):

        @pl.when((r + d) % REP // 2 == 4)
        def _():
            rse(d).start()

    for load in loads[3:]:
        load.wait()
    for k in range(REP):
        for t in range(SLOT):
            if t < WIDTHS[k]:
                slots_m[k, t] = tile_of(vmw, vmd, vme, STARTS[k] + t)
            else:
                slots_m[k, t] = jnp.zeros((ROWS, LANES), F32)

    def rows_of(shard):
        return pl.ds(pl.multiple_of(shard * ROWS, 8), ROWS)

    my_rows = rows_of(s)

    def reduce_tile(t):
        total = send[r, t].astype(F32)
        for d in range(1, REP):
            total = total + recv[d, t].astype(F32)
        momentum = MOMENTUM * slots_m[r, t] + total
        gall[r, t] = total.astype(BF16)
        x[t, my_rows, :] = (total + MOMENTUM * momentum).astype(BF16)

    def z_from(d):
        return (z - d + CHIPS_Z) % CHIPS_Z * 2 + c

    def z_to(d):
        return (z + d) % CHIPS_Z * 2 + c

    def zc(d, chunk):
        ref = x.at[tiles(chunk), my_rows, :]
        return rcopy(ref, ref, z_s.at[chunk, d], z_r.at[chunk, d], (r, z_to(d)))

    def zce(d):
        ref = x.at[4, my_rows, :]
        return rcopy(ref, ref, ze_s.at[d], ze_r.at[d], (r, z_to(d)))

    def fc(d, chunk):
        ref = x.at[tiles(chunk), rows_of(z_from(d)), :]
        return rcopy(ref, ref, f_s.at[chunk, d], f_r.at[chunk, d], (r, partner))

    def fce(d):
        ref = x.at[4, rows_of(z_from(d)), :]
        return rcopy(ref, ref, fe_s.at[d], fe_r.at[d], (r, partner))

    near = (1, 7, 2, 6, 3, 5, 4)
    for chunk in range(2):
        for d in range(1, REP):
            rs(d, chunk).wait_recv()
        for t in (2 * chunk, 2 * chunk + 1):
            reduce_tile(t)
        for d in near:
            zc(d, chunk).start()
        fc(0, chunk).start()

    @pl.when(five)
    def _():
        for d in range(1, REP):
            rse(d).wait_recv()
        reduce_tile(4)
        for d in near:
            zce(d).start()
        fce(0).start()

    def ga(d):
        ref = gall.at[r, 0:4]
        return rcopy(ref, ref, ga_s.at[d], ga_r.at[d], ((r + d) % REP, s))

    def gae(d):
        ref = gall.at[r, 4]
        return rcopy(ref, ref, gae_s.at[d], gae_r.at[d], ((r + d) % REP, s))

    for d in range(1, REP):
        ga(d).start()

        @pl.when(five)
        def _():
            gae(d).start()

    for chunk in range(2):
        for d in near:
            zc(d, chunk).wait_recv()
            fc(d, chunk).start()

    @pl.when(five)
    def _():
        for d in near:
            zce(d).wait_recv()
            fce(d).start()

    for chunk in range(2):
        for d in range(CHIPS_Z):
            fc(d, chunk).wait_recv()

    @pl.when(five)
    def _():
        for d in range(CHIPS_Z):
            fce(d).wait_recv()

    whole_x = jnp.concatenate([x[t] for t in range(SLOT)], axis=1)
    mine = []
    blocks = []
    for j in range(GROUPS):
        g = s * GROUPS + j
        block = g // 16
        row_block = jnp.where(block < 3, 0, jnp.where(block < 5, 1, 2))
        column_block = jnp.where(block < 3, block, jnp.where(block < 5, block - 2, 2))
        start = pl.multiple_of(row_block * LANES + g % 16 * 8, 8)
        mine.append(jnp.concatenate([x[t, pl.ds(start, 8), :] for t in range(SLOT)], axis=1))
        blocks.append(column_block)
    gram = lax.dot_general(
        jnp.concatenate(mine, axis=0), whole_x, (((1,), (1,)), ((), ())), preferred_element_type=F32
    )
    for j in range(GROUPS):
        rows = gram[8 * j : 8 * j + 8]
        part[8 * j : 8 * j + 8, :] = jnp.where(
            blocks[j] == 0,
            rows[:, :LANES],
            jnp.where(blocks[j] == 1, rows[:, LANES : 2 * LANES], rows[:, 2 * LANES :]),
        )

    first = jnp.where(r // 4 == 2, 8, r // 4 * 4)
    count = jnp.where(r // 4 == 2, 4, 3)
    embed = jnp.logical_or(r == 7, r == 15)
    count = jnp.where(embed, 2, jnp.where(r == 3, 1, count))

    def member(d):
        place = r - first + d
        inside = first + jnp.where(place >= count, place - count, place)
        return jnp.where(embed, (r + 8) % REP, inside)

    def gr(d):
        return rcopy(part, group.at[d], gr_s.at[d], gr_r.at[d], (member(d), s))

    for d in range(1, 4):

        @pl.when(d < count)
        def _():
            gr(d).start()

    def share(shard):
        return pl.ds(pl.multiple_of(shard * (8 * GROUPS), 8), 8 * GROUPS)

    my_share = share(s)
    tri[my_share, :] = part[...]
    for d in range(1, 4):

        @pl.when(d < count)
        def _():
            gr(d).wait_recv()
            tri[my_share, :] = tri[my_share, :] + group[d]

    def az(d):
        ref = tri.at[my_share, :]
        return rcopy(ref, ref, az_s.at[d], az_r.at[d], (r, z_to(d)))

    def af(d):
        ref = tri.at[share(z_from(d)), :]
        return rcopy(ref, ref, af_s.at[d], af_r.at[d], (r, partner))

    for d in near:
        az(d).start()
    af(0).start()

    for d in range(1, REP):
        ga(d).wait_recv()

        @pl.when((r - d + REP) % REP // 2 == 4)
        def _():
            src = (r - d + REP) % REP
            ref = gall.at[src, 4]
            rcopy(ref, ref, gae_s.at[d], gae_r.at[d], (src, s)).wait_recv()

    for k in range(REP):
        for t in range(WIDTHS[k]):
            put_tile(ow, od, oe, STARTS[k] + t, MOMENTUM * slots_m[k, t] + gall[k, t].astype(F32))

    for d in near:
        az(d).wait_recv()
        af(d).start()
    for d in range(CHIPS_Z):
        af(d).wait_recv()

    b0, b1, b2, b3, b4, b5 = (tri[b * LANES : (b + 1) * LANES, :] for b in range(6))
    a = jnp.concatenate(
        [
            jnp.concatenate([b0, b1, b2], axis=1),
            jnp.concatenate([b1.T, b3, b4], axis=1),
            jnp.concatenate([b2.T, b4.T, b5], axis=1),
        ],
        axis=0,
    )
    row = lax.broadcasted_iota(jnp.int32, (LANES, LANES), 0)
    column = lax.broadcasted_iota(jnp.int32, (LANES, LANES), 1)
    diagonal = jnp.where(row == column, b0 + b3 + b5, 0.0)
    trace = jnp.sum(jnp.sum(diagonal, axis=0, keepdims=True), axis=1, keepdims=True)
    scale = 1.0 / (jnp.sqrt(trace) + EPSILON)
    a = a * scale * scale

    lane = lax.broadcasted_iota(jnp.int32, (D, LANES), 1)
    q = jnp.where(
        jnp.logical_and(lax.broadcasted_iota(jnp.int32, (D, LANES), 0) - s * ROWS == lane, lane < ROWS), 1.0, 0.0
    )

    def pair(value):
        return jnp.concatenate(split(value), axis=1)

    def twice(value):
        return jnp.concatenate([value, value], axis=0)

    def packed(value):
        high = value.astype(BF16).astype(F32)
        return (high + pltpu.roll(value - high, LANES // 2, 1)).astype(BF16)

    def folded(value):
        return jnp.where(lane < LANES // 2, value + pltpu.roll(value, LANES // 2, 1), 0.0)

    for step in range(NS_ITERS):
        left = pair(a)
        if step < NS_ITERS - 1:
            right = twice(jnp.concatenate([a.astype(BF16), packed(q)], axis=1))
            out = dot(left, right)
            a2, qa = out[:, :D], folded(out[:, D:])
            out = dot(pair(a2), right)
            a3, qa2 = out[:, :D], folded(out[:, D:])
            b = COEF_A * a + COEF_B * a2 + COEF_C * a3
            a = COEF_A * b + dot(pair(COEF_B * a + COEF_C * a2), twice(b.astype(BF16)))
        else:
            qa = folded(dot(left, twice(packed(q))))
            qa2 = folded(dot(left, twice(packed(qa))))
        q = COEF_A * q + COEF_B * qa + COEF_C * qa2

    factor = jnp.float32(0.0)
    for k in range(REP):
        factor = factor + jnp.where(r == k, jnp.float32(math.sqrt(max(D, FACTORS[k]))), jnp.float32(0.0))
    whole_x = jnp.concatenate([x[t] for t in range(SLOT)], axis=1)
    result = (dot(q.T[:ROWS].astype(BF16), whole_x) * (scale * factor)).astype(BF16)
    for t in range(SLOT):
        upd[r, t] = result[:, t * LANES : (t + 1) * LANES]

    def up(d):
        ref = upd.at[r, 0:4]
        return rcopy(ref, ref, up_s.at[d], up_r.at[d], ((r + d) % REP, s))

    def upe(d):
        ref = upd.at[r, 4]
        return rcopy(ref, ref, upe_s.at[d], upe_r.at[d], ((r + d) % REP, s))

    for d in range(1, REP):
        up(d).start()

        @pl.when(five)
        def _():
            upe(d).start()

    for d in range(1, REP):
        for chunk in range(2):
            rs(d, chunk).wait_send()
        ga(d).wait_send()

        @pl.when((r + d) % REP // 2 == 4)
        def _():
            rse(d).wait_send()

        @pl.when(five)
        def _():
            gae(d).wait_send()

    for d in range(CHIPS_Z):
        for chunk in range(2):
            if d:
                zc(d, chunk).wait_send()
            fc(d, chunk).wait_send()
        if d:
            az(d).wait_send()
        af(d).wait_send()

        @pl.when(five)
        def _():
            if d:
                zce(d).wait_send()
            fce(d).wait_send()

    for d in range(1, 4):

        @pl.when(d < count)
        def _():
            gr(d).wait_send()

    for d in range(1, REP):
        up(d).wait_recv()

        @pl.when((r - d + REP) % REP // 2 == 4)
        def _():
            src = (r - d + REP) % REP
            ref = upd.at[src, 4]
            rcopy(ref, ref, upe_s.at[d], upe_r.at[d], (src, s)).wait_recv()

    for k in range(REP):
        for t in range(WIDTHS[k]):
            put_tile(uw, ud, ue, STARTS[k] + t, upd[k, t])
    for d in range(1, REP):
        up(d).wait_send()

        @pl.when(five)
        def _():
            upe(d).wait_send()


def store_kernel(*refs):
    sources, targets, sem = refs[:6], refs[6:12], refs[12]
    copies = [pltpu.make_async_copy(a, b, sem.at[i]) for i, (a, b) in enumerate(zip(sources, targets))]
    for copy in copies:
        copy.start()
    for copy in copies:
        copy.wait()


def per_device(grad_wide, grad_down, grad_embed, mom_wide, mom_down, mom_embed):
    shapes = [(ROWS, WIDE), (ROWS, DOWN), (ROWS, EMBED)]
    dma = pltpu.SemaphoreType.DMA
    scratch = (
        [pltpu.VMEM(shape, F32) for shape in shapes] * 2
        + [
            pltpu.VMEM((REP, SLOT, ROWS, LANES), BF16),
            pltpu.VMEM((REP, SLOT, ROWS, LANES), BF16),
            pltpu.VMEM((REP, SLOT, ROWS, LANES), F32),
            pltpu.VMEM((SLOT, D, LANES), BF16),
            pltpu.VMEM((REP, SLOT, ROWS, LANES), BF16),
            pltpu.VMEM((8 * GROUPS, LANES), F32),
            pltpu.VMEM((4, 8 * GROUPS, LANES), F32),
            pltpu.VMEM((6 * LANES, LANES), F32),
            pltpu.VMEM((REP, SLOT, ROWS, LANES), BF16),
        ]
        + [dma((6,))]
        + [dma((2, REP))] * 2
        + [dma((REP,))] * 6
        + [dma((2, CHIPS_Z))] * 2
        + [dma((CHIPS_Z,))] * 2
        + [dma((2, CHIPS_Z))] * 2
        + [dma((CHIPS_Z,))] * 2
        + [dma((4,))] * 2
        + [dma((CHIPS_Z,))] * 4
        + [dma((REP,))] * 4
    )
    outs = pl.pallas_call(
        kernel,
        out_shape=[jax.ShapeDtypeStruct(shape, F32) for shape in shapes]
        + [jax.ShapeDtypeStruct(shape, BF16) for shape in shapes],
        in_specs=[pl.BlockSpec(memory_space=pltpu.HBM)] * 6,
        out_specs=[pl.BlockSpec(memory_space=pltpu.VMEM)] * 6,
        scratch_shapes=scratch,
        compiler_params=pltpu.CompilerParams(
            collective_id=0, has_side_effects=True, vmem_limit_bytes=32 * 1024 * 1024
        ),
        name="muon",
    )(
        *[
            pltpu.with_memory_space_constraint(value, pltpu.HBM)
            for value in (
                grad_wide[0, 0],
                grad_down[0, 0].T,
                grad_embed[0].T,
                mom_wide[0],
                mom_down[0].T,
                mom_embed.T,
            )
        ]
    )
    outs = pl.pallas_call(
        store_kernel,
        out_shape=[jax.ShapeDtypeStruct(o.shape, o.dtype) for o in outs],
        in_specs=[pl.BlockSpec(memory_space=pl.ANY)] * 6,
        out_specs=[pl.BlockSpec(memory_space=pltpu.HBM)] * 6,
        scratch_shapes=[dma((6,))],
        compiler_params=pltpu.CompilerParams(vmem_limit_bytes=1024 * 1024),
        name="store",
    )(*outs)
    new_wide, new_down, new_embed, upd_wide, upd_down, upd_embed = outs
    return (
        new_wide[None],
        new_down.T[None],
        new_embed.T,
        upd_wide[None],
        upd_down.T[None],
        upd_embed.T,
    )


def solution(mesh):
    return jax.shard_map(
        per_device,
        mesh=mesh,
        in_specs=(
            P("rep", None, "shard", None),
            P("rep", None, None, "shard"),
            P("rep", None, "shard"),
            P(None, "shard", None),
            P(None, None, "shard"),
            P(None, "shard"),
        ),
        out_specs=(
            P(None, "shard", None),
            P(None, None, "shard"),
            P(None, "shard"),
        )
        * 2,
        check_vma=False,
    )
```

```python
import math

import jax
import jax.numpy as jnp
from jax import lax
from jax.experimental import pallas as pl
from jax.experimental.pallas import tpu as pltpu
from jax.sharding import PartitionSpec as P

D = 384
COEF_A = 3.4445
COEF_B = -4.775
COEF_C = 2.0315
MOMENTUM = 0.95
EPSILON = 1e-07
NS_ITERS = 5

REP = 16
SHARD = 16
CHIPS_Z = 8
ROWS = D // SHARD
LANES = 128
WIDE, DOWN, EMBED = 5376, 1536, 1001
TILES = 62
SLOT = 5
GROUPS = 6
CHUNKS = tuple((tile, 1) for tile in range(SLOT))
FAR = ((2, 2), (2, 1), (1, 2), (2, 3), (3, 2), (1, 1), (3, 3), (1, 3), (3, 1), (2, 0), (0, 2), (1, 0), (3, 0), (0, 1), (0, 3))
STARTS = (0, 3, 6, 9, 12, 16, 20, 54, 24, 29, 34, 38, 42, 46, 50, 58)
WIDTHS = (3, 3, 3, 3, 4, 4, 4, 4, 5, 5, 4, 4, 4, 4, 4, 4)
FACTORS = (1152, 1152, 1152, 384, 1536, 1536, 1536, 1001) + (2304,) * 4 + (1536,) * 3 + (1001,)
MESH = pl.DeviceIdType.MESH
BF16 = jnp.bfloat16
F32 = jnp.float32


def tile_of(wide, down, embed, tile):
    if tile < 42:
        return wide[:, tile * LANES : (tile + 1) * LANES]
    if tile < 54:
        return down[:, (tile - 42) * LANES : (tile - 41) * LANES]
    first = (tile - 54) * LANES
    if tile < 61:
        return embed[:, first : first + LANES]
    part = embed[:, first:EMBED]
    return jnp.concatenate([part, jnp.zeros((ROWS, first + LANES - EMBED), part.dtype)], axis=1)


def put_tile(wide, down, embed, tile, value):
    if tile < 42:
        wide[:, tile * LANES : (tile + 1) * LANES] = value
    elif tile < 54:
        down[:, (tile - 42) * LANES : (tile - 41) * LANES] = value
    else:
        first = (tile - 54) * LANES
        width = min(LANES, EMBED - first)
        embed[:, first : first + width] = value[:, :width]


def split(value):
    high = value.astype(BF16)
    return high, (value - high.astype(F32)).astype(BF16)


def dot(left, right):
    return jnp.dot(left, right, preferred_element_type=F32)


def kernel(
    gw, gd, ge, mw, md, me_,
    ow, od, oe, uw, ud, ue,
    vgw, vgd, vge, vmw, vmd, vme,
    send, recv, slots_m, x, gall, part, group, tri, upd,
    load_sem, rs_s, rs_r, ga_s, ga_r, gae_s, gae_r, z_s, z_r, f_s, f_r, gr_s, gr_r, az_s, az_r, af_s, af_r,
    up_s, up_r, upe_s, upe_r,
):
    r = lax.axis_index("rep")
    s = lax.axis_index("shard")
    z = s // 2
    c = s % 2
    partner = z * 2 + (1 - c)
    five = r // 2 == 4

    def rep_to(d):
        return (r // 4 + FAR[d - 1][1]) % 4 * 4 + (r + FAR[d - 1][0]) % 4

    barrier = pltpu.get_barrier_semaphore()

    def greet(device):
        pl.semaphore_signal(barrier, inc=1, device_id=device, device_id_type=MESH)

    for d in (4, 3, 5, 2, 6, 1, 7):
        greet((r, (z + d) % CHIPS_Z * 2 + c))
    for d in range(1, REP):
        greet((rep_to(d), s))
    greet((r, partner))

    loads = [
        pltpu.make_async_copy(a, b, load_sem.at[i])
        for i, (a, b) in enumerate(((gw, vgw), (gd, vgd), (ge, vge), (mw, vmw), (md, vmd), (me_, vme)))
    ]
    for load in loads:
        load.start()

    for load in loads[:3]:
        load.wait()
    for k in range(REP):
        for t in range(SLOT):
            if t < WIDTHS[k]:
                send[k, t] = tile_of(vgw, vgd, vge, STARTS[k] + t).astype(BF16)
            else:
                send[k, t] = jnp.zeros((ROWS, LANES), BF16)

    pl.semaphore_wait(barrier, REP - 1 + CHIPS_Z - 1 + 1)

    def rcopy(src, dst, ss, rs, device):
        return pltpu.make_async_remote_copy(
            src_ref=src, dst_ref=dst, send_sem=ss, recv_sem=rs, device_id=device, device_id_type=MESH
        )

    def settle(ref, sem):
        rcopy(ref, ref, sem, sem, (r, partner)).wait_recv()

    def when_held(chunk, condition, body):
        if CHUNKS[chunk][0] == SLOT - 1:
            pl.when(condition)(body)
        else:
            body()

    def tiles(chunk):
        return pl.ds(*CHUNKS[chunk])

    def rs(d, chunk):
        to = rep_to(d)
        return rcopy(send.at[to, tiles(chunk)], recv.at[d, tiles(chunk)], rs_s.at[chunk // 4], rs_r.at[chunk], (to, s))

    for chunk in range(len(CHUNKS)):
        for d in range(1, REP):
            when_held(chunk, rep_to(d) // 2 == 4, rs(d, chunk).start)

    for load in loads[3:]:
        load.wait()
    for k in range(REP):
        for t in range(SLOT):
            if t < WIDTHS[k]:
                slots_m[k, t] = tile_of(vmw, vmd, vme, STARTS[k] + t)
            else:
                slots_m[k, t] = jnp.zeros((ROWS, LANES), F32)

    @pl.when(jnp.logical_not(five))
    def _():
        x[SLOT - 1] = jnp.zeros((D, LANES), BF16)

    def rows_of(shard):
        return pl.ds(pl.multiple_of(shard * ROWS, 8), ROWS)

    my_rows = rows_of(s)

    def reduce_tile(t):
        total = send[r, t].astype(F32)
        for d in range(1, REP):
            total = total + recv[d, t].astype(F32)
        momentum = MOMENTUM * slots_m[r, t] + total
        gall[r, t] = total.astype(BF16)
        x[t, my_rows, :] = (total + MOMENTUM * momentum).astype(BF16)

    def z_from(d):
        return (z - d + CHIPS_Z) % CHIPS_Z * 2 + c

    def z_to(d):
        return (z + d) % CHIPS_Z * 2 + c

    def zc(d, chunk):
        ref = x.at[tiles(chunk), my_rows, :]
        return rcopy(ref, ref, z_s.at[chunk // 4], z_r.at[chunk], (r, z_to(d)))

    def fc(d, chunk):
        ref = x.at[tiles(chunk), rows_of(z_from(d)), :]
        return rcopy(ref, ref, f_s.at[chunk // 4], f_r.at[chunk], (r, partner))

    far = (4, 3, 5, 2, 6, 1, 7)

    def scatter(chunk):
        settle(recv.at[pl.ds(1, REP - 1), tiles(chunk)], rs_r.at[chunk])
        start, size = CHUNKS[chunk]
        for t in range(start, start + size):
            reduce_tile(t)
        for d in far:
            zc(d, chunk).start()

    def forward(chunk):
        settle(x.at[tiles(chunk), pl.ds(0, (CHIPS_Z - 1) * ROWS), :], z_r.at[chunk])
        for d in range(CHIPS_Z):
            fc(d, chunk).start()

    for chunk in range(len(CHUNKS)):
        when_held(chunk, five, lambda chunk=chunk: scatter(chunk))

    def spread(buffer, send_sem, recv_sem, extra_send, extra_recv):
        for d in range(1, REP):
            ref = buffer.at[r, 0:4]
            rcopy(ref, ref, send_sem, recv_sem, (rep_to(d), s)).start()

        @pl.when(five)
        def _():
            for d in range(1, REP):
                ref = buffer.at[r, 4:5]
                rcopy(ref, ref, extra_send, extra_recv, (rep_to(d), s)).start()

    def spread_arrived(buffer, recv_sem, extra_recv):
        settle(buffer.at[0 : REP - 1, 0:4], recv_sem)

        @pl.when(five)
        def _():
            settle(buffer.at[8:9, 4:5], extra_recv)

        @pl.when(jnp.logical_not(five))
        def _():
            settle(buffer.at[8:10, 4:5], extra_recv)

    def spread_sent(buffer, send_sem, extra_send):
        settle(buffer.at[0 : REP - 1, 0:4], send_sem)

        @pl.when(five)
        def _():
            settle(buffer.at[0 : REP - 1, 4:5], extra_send)

    spread(gall, ga_s, ga_r, gae_s, gae_r)

    for chunk in range(len(CHUNKS)):
        when_held(chunk, five, lambda chunk=chunk: forward(chunk))

    def whole(chunk):
        return x.at[tiles(chunk), pl.ds(0, CHIPS_Z * ROWS), :]

    for chunk in range(len(CHUNKS)):
        when_held(chunk, five, lambda chunk=chunk: settle(whole(chunk), f_r.at[chunk]))

    whole_x = jnp.concatenate([x[t] for t in range(SLOT)], axis=1)
    mine = []
    blocks = []
    for j in range(GROUPS):
        g = s * GROUPS + j
        block = g // 16
        row_block = jnp.where(block < 3, 0, jnp.where(block < 5, 1, 2))
        column_block = jnp.where(block < 3, block, jnp.where(block < 5, block - 2, 2))
        start = pl.multiple_of(row_block * LANES + g % 16 * 8, 8)
        mine.append(jnp.concatenate([x[t, pl.ds(start, 8), :] for t in range(SLOT)], axis=1))
        blocks.append(column_block)
    gram = lax.dot_general(
        jnp.concatenate(mine, axis=0), whole_x, (((1,), (1,)), ((), ())), preferred_element_type=F32
    )
    for j in range(GROUPS):
        rows = gram[8 * j : 8 * j + 8]
        part[8 * j : 8 * j + 8, :] = jnp.where(
            blocks[j] == 0,
            rows[:, :LANES],
            jnp.where(blocks[j] == 1, rows[:, LANES : 2 * LANES], rows[:, 2 * LANES :]),
        )

    first = jnp.where(r // 4 == 2, 8, r // 4 * 4)
    count = jnp.where(r // 4 == 2, 4, 3)
    embed = jnp.logical_or(r == 7, r == 15)
    count = jnp.where(embed, 2, jnp.where(r == 3, 1, count))

    def member(d):
        place = r - first + d
        inside = first + jnp.where(place >= count, place - count, place)
        return jnp.where(embed, (r + 8) % REP, inside)

    def gr(d):
        return rcopy(part, group.at[d], gr_s.at[d], gr_r.at[d], (member(d), s))

    for d in range(1, 4):

        @pl.when(d < count)
        def _():
            gr(d).start()

    def share(shard):
        return pl.ds(pl.multiple_of(shard * (8 * GROUPS), 8), 8 * GROUPS)

    my_share = share(s)
    tri[my_share, :] = part[...]
    for d in range(1, 4):

        @pl.when(d < count)
        def _():
            gr(d).wait_recv()
            tri[my_share, :] = tri[my_share, :] + group[d]

    def az(d):
        ref = tri.at[my_share, :]
        return rcopy(ref, ref, az_s, az_r.at[d], (r, z_to(d)))

    def af(d):
        ref = tri.at[share(z_from(d)), :]
        return rcopy(ref, ref, af_s, af_r, (r, partner))

    for d in far:
        az(d).start()
    af(0).start()

    spread_arrived(gall, ga_r, gae_r)
    for k in range(REP):
        for t in range(WIDTHS[k]):
            put_tile(ow, od, oe, STARTS[k] + t, MOMENTUM * slots_m[k, t] + gall[k, t].astype(F32))

    for d in far:
        az(d).wait_recv()
        af(d).start()
    settle(tri.at[pl.ds(0, 3 * LANES), :], af_r)

    b0, b1, b2, b3, b4, b5 = (tri[b * LANES : (b + 1) * LANES, :] for b in range(6))
    a = jnp.concatenate(
        [
            jnp.concatenate([b0, b1, b2], axis=1),
            jnp.concatenate([b1.T, b3, b4], axis=1),
            jnp.concatenate([b2.T, b4.T, b5], axis=1),
        ],
        axis=0,
    )
    row = lax.broadcasted_iota(jnp.int32, (LANES, LANES), 0)
    column = lax.broadcasted_iota(jnp.int32, (LANES, LANES), 1)
    diagonal = jnp.where(row == column, b0 + b3 + b5, 0.0)
    trace = jnp.sum(jnp.sum(diagonal, axis=0, keepdims=True), axis=1, keepdims=True)
    scale = 1.0 / (jnp.sqrt(trace) + EPSILON)
    a = a * scale * scale

    lane = lax.broadcasted_iota(jnp.int32, (D, LANES), 1)
    q = jnp.where(
        jnp.logical_and(lax.broadcasted_iota(jnp.int32, (D, LANES), 0) - s * ROWS == lane, lane < ROWS), 1.0, 0.0
    )

    def twice(value):
        high = value.astype(BF16)
        return jnp.concatenate([high, high], axis=1)

    for step in range(NS_ITERS):
        qh, ql = split(q)
        ah, al = split(a)
        if step < NS_ITERS - 1:
            right = jnp.concatenate(
                [jnp.concatenate([ah, qh], axis=1), jnp.concatenate([al, ql], axis=1)], axis=0
            )
            out = dot(jnp.concatenate([ah, ah], axis=1), right)
            a2, qa = out[:, :D], out[:, D:]
            out = dot(twice(a2), right)
            a3, qa2 = out[:, :D], out[:, D:]
            b = COEF_A * a + COEF_B * a2 + COEF_C * a3
            a = COEF_A * b + dot(
                twice(COEF_B * a + COEF_C * a2), jnp.concatenate(split(b), axis=0)
            )
        else:
            left = jnp.concatenate([ah, al], axis=1)

            def times(high, low):
                both = jnp.concatenate([high, low], axis=1)
                out = dot(left, jnp.concatenate([both, both], axis=0))
                return out[:, :LANES] + out[:, LANES:]

            qa = times(qh, ql)
            qa2 = times(*split(qa))
        q = COEF_A * q + COEF_B * qa + COEF_C * qa2

    factor = jnp.float32(0.0)
    for k in range(REP):
        factor = factor + jnp.where(r == k, jnp.float32(math.sqrt(max(D, FACTORS[k]))), jnp.float32(0.0))
    whole_x = jnp.concatenate([x[t] for t in range(SLOT)], axis=1)
    result = (dot(q.T[:ROWS].astype(BF16), whole_x) * (scale * factor)).astype(BF16)
    for t in range(SLOT):
        upd[r, t] = result[:, t * LANES : (t + 1) * LANES]

    spread(upd, up_s, up_r, upe_s, upe_r)

    spread_sent(gall, ga_s, gae_s)
    settle(send.at[0 : REP - 1, 0:4], rs_s.at[0])
    settle(x.at[0:4, pl.ds(0, (CHIPS_Z - 1) * ROWS), :], z_s.at[0])
    settle(x.at[0:4, pl.ds(0, CHIPS_Z * ROWS), :], f_s.at[0])

    @pl.when(five)
    def _():
        settle(send.at[0:1, 4:5], rs_s.at[1])
        settle(x.at[4:5, pl.ds(0, (CHIPS_Z - 1) * ROWS), :], z_s.at[1])
        settle(x.at[4:5, pl.ds(0, CHIPS_Z * ROWS), :], f_s.at[1])

    @pl.when(jnp.logical_not(five))
    def _():
        settle(send.at[0:2, 4:5], rs_s.at[1])

    settle(tri.at[pl.ds(0, (CHIPS_Z - 1) * 8 * GROUPS), :], az_s)
    settle(tri.at[pl.ds(0, 3 * LANES), :], af_s)
    for d in range(1, 4):

        @pl.when(d < count)
        def _():
            gr(d).wait_send()

    spread_arrived(upd, up_r, upe_r)
    for k in range(REP):
        for t in range(WIDTHS[k]):
            put_tile(uw, ud, ue, STARTS[k] + t, upd[k, t])
    spread_sent(upd, up_s, upe_s)


def store_kernel(*refs):
    sources, targets, sem = refs[:6], refs[6:12], refs[12]
    copies = [pltpu.make_async_copy(a, b, sem.at[i]) for i, (a, b) in enumerate(zip(sources, targets))]
    for copy in copies:
        copy.start()
    for copy in copies:
        copy.wait()


def per_device(grad_wide, grad_down, grad_embed, mom_wide, mom_down, mom_embed):
    shapes = [(ROWS, WIDE), (ROWS, DOWN), (ROWS, EMBED)]
    dma = pltpu.SemaphoreType.DMA
    scratch = (
        [pltpu.VMEM(shape, F32) for shape in shapes] * 2
        + [
            pltpu.VMEM((REP, SLOT, ROWS, LANES), BF16),
            pltpu.VMEM((REP, SLOT, ROWS, LANES), BF16),
            pltpu.VMEM((REP, SLOT, ROWS, LANES), F32),
            pltpu.VMEM((SLOT, D, LANES), BF16),
            pltpu.VMEM((REP, SLOT, ROWS, LANES), BF16),
            pltpu.VMEM((8 * GROUPS, LANES), F32),
            pltpu.VMEM((4, 8 * GROUPS, LANES), F32),
            pltpu.VMEM((6 * LANES, LANES), F32),
            pltpu.VMEM((REP, SLOT, ROWS, LANES), BF16),
        ]
        + [dma((6,))]
        + [dma((2,)), dma((len(CHUNKS),))]
        + [dma(())] * 4
        + [dma((2,)), dma((len(CHUNKS),))] * 2
        + [dma((4,))] * 2
        + [dma(()), dma((CHIPS_Z,)), dma(()), dma(())]
        + [dma(())] * 4
    )
    outs = pl.pallas_call(
        kernel,
        out_shape=[jax.ShapeDtypeStruct(shape, F32) for shape in shapes]
        + [jax.ShapeDtypeStruct(shape, BF16) for shape in shapes],
        in_specs=[pl.BlockSpec(memory_space=pltpu.HBM)] * 6,
        out_specs=[pl.BlockSpec(memory_space=pltpu.VMEM)] * 6,
        scratch_shapes=scratch,
        compiler_params=pltpu.CompilerParams(
            collective_id=0, has_side_effects=True, vmem_limit_bytes=32 * 1024 * 1024
        ),
        name="muon",
    )(
        *[
            pltpu.with_memory_space_constraint(value, pltpu.HBM)
            for value in (
                grad_wide[0, 0],
                grad_down[0, 0].T,
                grad_embed[0].T,
                mom_wide[0],
                mom_down[0].T,
                mom_embed.T,
            )
        ]
    )
    outs = pl.pallas_call(
        store_kernel,
        out_shape=[jax.ShapeDtypeStruct(o.shape, o.dtype) for o in outs],
        in_specs=[pl.BlockSpec(memory_space=pl.ANY)] * 6,
        out_specs=[pl.BlockSpec(memory_space=pltpu.HBM)] * 6,
        scratch_shapes=[dma((6,))],
        compiler_params=pltpu.CompilerParams(vmem_limit_bytes=1024 * 1024),
        name="store",
    )(*outs)
    new_wide, new_down, new_embed, upd_wide, upd_down, upd_embed = outs
    return (
        new_wide[None],
        new_down.T[None],
        new_embed.T,
        upd_wide[None],
        upd_down.T[None],
        upd_embed.T,
    )


def solution(mesh):
    return jax.shard_map(
        per_device,
        mesh=mesh,
        in_specs=(
            P("rep", None, "shard", None),
            P("rep", None, None, "shard"),
            P("rep", None, "shard"),
            P(None, "shard", None),
            P(None, None, "shard"),
            P(None, "shard"),
        ),
        out_specs=(
            P(None, "shard", None),
            P(None, None, "shard"),
            P(None, "shard"),
        )
        * 2,
        check_vma=False,
    )
```

```python
import math

import jax
import jax.numpy as jnp
from jax import lax
from jax.experimental import pallas as pl
from jax.experimental.pallas import tpu as pltpu
from jax.sharding import PartitionSpec as P

D = 384
COEF_A = 3.4445
COEF_B = -4.775
COEF_C = 2.0315
MOMENTUM = 0.95
EPSILON = 1e-07
NS_ITERS = 5

REP = 16
SHARD = 16
CHIPS_Z = 8
ROWS = D // SHARD
LANES = 128
WIDE, DOWN, EMBED = 5376, 1536, 1001
TILES = 62
SLOT = 5
GROUPS = 6
CHUNKS = tuple((tile, 1) for tile in range(SLOT))
FAR = ((2, 2), (2, 1), (1, 2), (2, 3), (3, 2), (1, 1), (3, 3), (1, 3), (3, 1), (2, 0), (0, 2), (1, 0), (3, 0), (0, 1), (0, 3))
STARTS = (0, 3, 6, 9, 12, 16, 20, 54, 24, 29, 34, 38, 42, 46, 50, 58)
WIDTHS = (3, 3, 3, 3, 4, 4, 4, 4, 5, 5, 4, 4, 4, 4, 4, 4)
FACTORS = (1152, 1152, 1152, 384, 1536, 1536, 1536, 1001) + (2304,) * 4 + (1536,) * 3 + (1001,)
MESH = pl.DeviceIdType.MESH
BF16 = jnp.bfloat16
F32 = jnp.float32


def tile_of(wide, down, embed, tile):
    if tile < 42:
        return wide[:, tile * LANES : (tile + 1) * LANES]
    if tile < 54:
        return down[:, (tile - 42) * LANES : (tile - 41) * LANES]
    first = (tile - 54) * LANES
    if tile < 61:
        return embed[:, first : first + LANES]
    part = embed[:, first:EMBED]
    return jnp.concatenate([part, jnp.zeros((ROWS, first + LANES - EMBED), part.dtype)], axis=1)


def put_tile(wide, down, embed, tile, value):
    if tile < 42:
        wide[:, tile * LANES : (tile + 1) * LANES] = value
    elif tile < 54:
        down[:, (tile - 42) * LANES : (tile - 41) * LANES] = value
    else:
        first = (tile - 54) * LANES
        width = min(LANES, EMBED - first)
        embed[:, first : first + width] = value[:, :width]


def split(value):
    high = value.astype(BF16)
    return high, (value - high.astype(F32)).astype(BF16)


def dot(left, right):
    return jnp.dot(left, right, preferred_element_type=F32)


def kernel(
    gw, gd, ge, mw, md, me_,
    ow, od, oe, uw, ud, ue,
    vgw, vgd, vge, vmw, vmd, vme,
    send, recv, slots_m, x, gall, part, group, tri, upd,
    load_sem, rs_s, rs_r, ga_s, ga_r, gae_s, gae_r, z_s, z_r, f_s, f_r, gr_s, gr_r, az_s, az_r, af_s, af_r,
    up_s, up_r, upe_s, upe_r,
):
    r = lax.axis_index("rep")
    s = lax.axis_index("shard")
    z = s // 2
    c = s % 2
    partner = z * 2 + (1 - c)
    five = r // 2 == 4

    def rep_to(d):
        return (r // 4 + FAR[d - 1][1]) % 4 * 4 + (r + FAR[d - 1][0]) % 4

    barrier = pltpu.get_barrier_semaphore()

    def greet(device):
        pl.semaphore_signal(barrier, inc=1, device_id=device, device_id_type=MESH)

    for d in (4, 3, 5, 2, 6, 1, 7):
        greet((r, (z + d) % CHIPS_Z * 2 + c))
    for d in range(1, REP):
        greet((rep_to(d), s))
    greet((r, partner))

    loads = [
        pltpu.make_async_copy(a, b, load_sem.at[i])
        for i, (a, b) in enumerate(((gw, vgw), (gd, vgd), (ge, vge), (mw, vmw), (md, vmd), (me_, vme)))
    ]
    for load in loads:
        load.start()

    for load in loads[:3]:
        load.wait()
    for k in range(REP):
        for t in range(SLOT):
            if t < WIDTHS[k]:
                send[k, t] = tile_of(vgw, vgd, vge, STARTS[k] + t).astype(BF16)
            else:
                send[k, t] = jnp.zeros((ROWS, LANES), BF16)

    pl.semaphore_wait(barrier, REP - 1 + CHIPS_Z - 1 + 1)

    def rcopy(src, dst, ss, rs, device):
        return pltpu.make_async_remote_copy(
            src_ref=src, dst_ref=dst, send_sem=ss, recv_sem=rs, device_id=device, device_id_type=MESH
        )

    def settle(ref, sem):
        rcopy(ref, ref, sem, sem, (r, partner)).wait_recv()

    def when_held(chunk, condition, body):
        if CHUNKS[chunk][0] == SLOT - 1:
            pl.when(condition)(body)
        else:
            body()

    def tiles(chunk):
        return pl.ds(*CHUNKS[chunk])

    def rs(d, chunk):
        to = rep_to(d)
        return rcopy(send.at[to, tiles(chunk)], recv.at[d, tiles(chunk)], rs_s.at[chunk // 4], rs_r.at[chunk], (to, s))

    for chunk in range(len(CHUNKS)):
        for d in range(1, REP):
            when_held(chunk, rep_to(d) // 2 == 4, rs(d, chunk).start)

    for load in loads[3:]:
        load.wait()
    for k in range(REP):
        for t in range(SLOT):
            if t < WIDTHS[k]:
                slots_m[k, t] = tile_of(vmw, vmd, vme, STARTS[k] + t)
            else:
                slots_m[k, t] = jnp.zeros((ROWS, LANES), F32)

    @pl.when(jnp.logical_not(five))
    def _():
        x[SLOT - 1] = jnp.zeros((D, LANES), BF16)

    def rows_of(shard):
        return pl.ds(pl.multiple_of(shard * ROWS, 8), ROWS)

    my_rows = rows_of(s)

    def reduce_tile(t):
        total = send[r, t].astype(F32)
        for d in range(1, REP):
            total = total + recv[d, t].astype(F32)
        momentum = MOMENTUM * slots_m[r, t] + total
        gall[r, t] = total.astype(BF16)
        x[t, my_rows, :] = (total + MOMENTUM * momentum).astype(BF16)

    def z_from(d):
        return (z - d + CHIPS_Z) % CHIPS_Z * 2 + c

    def z_to(d):
        return (z + d) % CHIPS_Z * 2 + c

    def zc(d, chunk):
        ref = x.at[tiles(chunk), my_rows, :]
        return rcopy(ref, ref, z_s.at[chunk // 4], z_r.at[chunk], (r, z_to(d)))

    def fc(d, chunk):
        ref = x.at[tiles(chunk), rows_of(z_from(d)), :]
        return rcopy(ref, ref, f_s.at[chunk // 4], f_r.at[chunk], (r, partner))

    far = (4, 3, 5, 2, 6, 1, 7)

    def scatter(chunk):
        settle(recv.at[pl.ds(1, REP - 1), tiles(chunk)], rs_r.at[chunk])
        start, size = CHUNKS[chunk]
        for t in range(start, start + size):
            reduce_tile(t)
        for d in far:
            zc(d, chunk).start()

    def forward(chunk):
        settle(x.at[tiles(chunk), pl.ds(0, (CHIPS_Z - 1) * ROWS), :], z_r.at[chunk])
        for d in range(CHIPS_Z):
            fc(d, chunk).start()

    for chunk in range(len(CHUNKS)):
        when_held(chunk, five, lambda chunk=chunk: scatter(chunk))

    def spread(buffer, send_sem, recv_sem, extra_send, extra_recv):
        for d in range(1, REP):
            ref = buffer.at[r, 0:4]
            rcopy(ref, ref, send_sem, recv_sem, (rep_to(d), s)).start()

        @pl.when(five)
        def _():
            for d in range(1, REP):
                ref = buffer.at[r, 4:5]
                rcopy(ref, ref, extra_send, extra_recv, (rep_to(d), s)).start()

    def spread_arrived(buffer, recv_sem, extra_recv):
        settle(buffer.at[0 : REP - 1, 0:4], recv_sem)

        @pl.when(five)
        def _():
            settle(buffer.at[8:9, 4:5], extra_recv)

        @pl.when(jnp.logical_not(five))
        def _():
            settle(buffer.at[8:10, 4:5], extra_recv)

    def spread_sent(buffer, send_sem, extra_send):
        settle(buffer.at[0 : REP - 1, 0:4], send_sem)

        @pl.when(five)
        def _():
            settle(buffer.at[0 : REP - 1, 4:5], extra_send)

    spread(gall, ga_s, ga_r, gae_s, gae_r)

    for chunk in range(len(CHUNKS)):
        when_held(chunk, five, lambda chunk=chunk: forward(chunk))

    def whole(chunk):
        return x.at[tiles(chunk), pl.ds(0, CHIPS_Z * ROWS), :]

    for chunk in range(len(CHUNKS)):
        when_held(chunk, five, lambda chunk=chunk: settle(whole(chunk), f_r.at[chunk]))

    whole_x = jnp.concatenate([x[t] for t in range(SLOT)], axis=1)
    mine = []
    blocks = []
    for j in range(GROUPS):
        g = s * GROUPS + j
        block = g // 16
        row_block = jnp.where(block < 3, 0, jnp.where(block < 5, 1, 2))
        column_block = jnp.where(block < 3, block, jnp.where(block < 5, block - 2, 2))
        start = pl.multiple_of(row_block * LANES + g % 16 * 8, 8)
        mine.append(jnp.concatenate([x[t, pl.ds(start, 8), :] for t in range(SLOT)], axis=1))
        blocks.append(column_block)
    gram = lax.dot_general(
        jnp.concatenate(mine, axis=0), whole_x, (((1,), (1,)), ((), ())), preferred_element_type=F32
    )
    for j in range(GROUPS):
        rows = gram[8 * j : 8 * j + 8]
        part[8 * j : 8 * j + 8, :] = jnp.where(
            blocks[j] == 0,
            rows[:, :LANES],
            jnp.where(blocks[j] == 1, rows[:, LANES : 2 * LANES], rows[:, 2 * LANES :]),
        )

    first = jnp.where(r // 4 == 2, 8, r // 4 * 4)
    count = jnp.where(r // 4 == 2, 4, 3)
    embed = jnp.logical_or(r == 7, r == 15)
    count = jnp.where(embed, 2, jnp.where(r == 3, 1, count))

    def member(d):
        place = r - first + d
        inside = first + jnp.where(place >= count, place - count, place)
        return jnp.where(embed, (r + 8) % REP, inside)

    def gr(d):
        return rcopy(part, group.at[d], gr_s.at[d], gr_r.at[d], (member(d), s))

    for d in range(1, 4):

        @pl.when(d < count)
        def _():
            gr(d).start()

    def share(shard):
        return pl.ds(pl.multiple_of(shard * (8 * GROUPS), 8), 8 * GROUPS)

    my_share = share(s)
    tri[my_share, :] = part[...]
    for d in range(1, 4):

        @pl.when(d < count)
        def _():
            gr(d).wait_recv()
            tri[my_share, :] = tri[my_share, :] + group[d]

    def az(d):
        ref = tri.at[my_share, :]
        return rcopy(ref, ref, az_s, az_r.at[d], (r, z_to(d)))

    def af(d):
        ref = tri.at[share(z_from(d)), :]
        return rcopy(ref, ref, af_s, af_r, (r, partner))

    for d in far:
        az(d).start()
    af(0).start()

    spread_arrived(gall, ga_r, gae_r)
    for k in range(REP):
        for t in range(WIDTHS[k]):
            put_tile(ow, od, oe, STARTS[k] + t, MOMENTUM * slots_m[k, t] + gall[k, t].astype(F32))

    for d in far:
        az(d).wait_recv()
        af(d).start()
    settle(tri.at[pl.ds(0, 3 * LANES), :], af_r)

    b0, b1, b2, b3, b4, b5 = (tri[b * LANES : (b + 1) * LANES, :] for b in range(6))
    a = jnp.concatenate(
        [
            jnp.concatenate([b0, b1, b2], axis=1),
            jnp.concatenate([b1.T, b3, b4], axis=1),
            jnp.concatenate([b2.T, b4.T, b5], axis=1),
        ],
        axis=0,
    )
    row = lax.broadcasted_iota(jnp.int32, (LANES, LANES), 0)
    column = lax.broadcasted_iota(jnp.int32, (LANES, LANES), 1)
    diagonal = jnp.where(row == column, b0 + b3 + b5, 0.0)
    trace = jnp.sum(jnp.sum(diagonal, axis=0, keepdims=True), axis=1, keepdims=True)
    scale = 1.0 / (jnp.sqrt(trace) + EPSILON)
    a = a * scale * scale

    lane = lax.broadcasted_iota(jnp.int32, (D, LANES), 1)
    q = jnp.where(
        jnp.logical_and(lax.broadcasted_iota(jnp.int32, (D, LANES), 0) - s * ROWS == lane, lane < ROWS), 1.0, 0.0
    )

    def product(value, right):
        high = value.astype(BF16)
        return dot(high if right.shape[0] == D else jnp.concatenate([high, high], axis=1), right)

    def stacked(value, fine):
        high, low = split(value)
        return jnp.concatenate([high, low], axis=0) if fine else high

    for step in range(NS_ITERS):
        if step < NS_ITERS - 1:
            fine = step >= 2
            right = jnp.concatenate([stacked(a, fine), stacked(q, fine)], axis=1)
            out = product(a, right)
            a2, qa = out[:, :D], out[:, D:]
            out = product(a2, right)
            a3, qa2 = out[:, :D], out[:, D:]
            b = COEF_A * a + COEF_B * a2 + COEF_C * a3
            a = COEF_A * b + product(COEF_B * a + COEF_C * a2, stacked(b, fine))
        else:
            qh, ql = split(q)
            left = jnp.concatenate(split(a), axis=1)

            def times(high, low):
                both = jnp.concatenate([high, low], axis=1)
                out = dot(left, jnp.concatenate([both, both], axis=0))
                return out[:, :LANES] + out[:, LANES:]

            qa = times(qh, ql)
            qa2 = times(*split(qa))
        q = COEF_A * q + COEF_B * qa + COEF_C * qa2

    factor = jnp.float32(0.0)
    for k in range(REP):
        factor = factor + jnp.where(r == k, jnp.float32(math.sqrt(max(D, FACTORS[k]))), jnp.float32(0.0))
    whole_x = jnp.concatenate([x[t] for t in range(SLOT)], axis=1)
    result = (dot(q.T[:ROWS].astype(BF16), whole_x) * (scale * factor)).astype(BF16)
    for t in range(SLOT):
        upd[r, t] = result[:, t * LANES : (t + 1) * LANES]

    spread(upd, up_s, up_r, upe_s, upe_r)

    spread_sent(gall, ga_s, gae_s)
    settle(send.at[0 : REP - 1, 0:4], rs_s.at[0])
    settle(x.at[0:4, pl.ds(0, (CHIPS_Z - 1) * ROWS), :], z_s.at[0])
    settle(x.at[0:4, pl.ds(0, CHIPS_Z * ROWS), :], f_s.at[0])

    @pl.when(five)
    def _():
        settle(send.at[0:1, 4:5], rs_s.at[1])
        settle(x.at[4:5, pl.ds(0, (CHIPS_Z - 1) * ROWS), :], z_s.at[1])
        settle(x.at[4:5, pl.ds(0, CHIPS_Z * ROWS), :], f_s.at[1])

    @pl.when(jnp.logical_not(five))
    def _():
        settle(send.at[0:2, 4:5], rs_s.at[1])

    settle(tri.at[pl.ds(0, (CHIPS_Z - 1) * 8 * GROUPS), :], az_s)
    settle(tri.at[pl.ds(0, 3 * LANES), :], af_s)
    for d in range(1, 4):

        @pl.when(d < count)
        def _():
            gr(d).wait_send()

    spread_arrived(upd, up_r, upe_r)
    for k in range(REP):
        for t in range(WIDTHS[k]):
            put_tile(uw, ud, ue, STARTS[k] + t, upd[k, t])
    spread_sent(upd, up_s, upe_s)


def store_kernel(*refs):
    sources, targets, sem = refs[:6], refs[6:12], refs[12]
    copies = [pltpu.make_async_copy(a, b, sem.at[i]) for i, (a, b) in enumerate(zip(sources, targets))]
    for copy in copies:
        copy.start()
    for copy in copies:
        copy.wait()


def per_device(grad_wide, grad_down, grad_embed, mom_wide, mom_down, mom_embed):
    shapes = [(ROWS, WIDE), (ROWS, DOWN), (ROWS, EMBED)]
    dma = pltpu.SemaphoreType.DMA
    scratch = (
        [pltpu.VMEM(shape, F32) for shape in shapes] * 2
        + [
            pltpu.VMEM((REP, SLOT, ROWS, LANES), BF16),
            pltpu.VMEM((REP, SLOT, ROWS, LANES), BF16),
            pltpu.VMEM((REP, SLOT, ROWS, LANES), F32),
            pltpu.VMEM((SLOT, D, LANES), BF16),
            pltpu.VMEM((REP, SLOT, ROWS, LANES), BF16),
            pltpu.VMEM((8 * GROUPS, LANES), F32),
            pltpu.VMEM((4, 8 * GROUPS, LANES), F32),
            pltpu.VMEM((6 * LANES, LANES), F32),
            pltpu.VMEM((REP, SLOT, ROWS, LANES), BF16),
        ]
        + [dma((6,))]
        + [dma((2,)), dma((len(CHUNKS),))]
        + [dma(())] * 4
        + [dma((2,)), dma((len(CHUNKS),))] * 2
        + [dma((4,))] * 2
        + [dma(()), dma((CHIPS_Z,)), dma(()), dma(())]
        + [dma(())] * 4
    )
    outs = pl.pallas_call(
        kernel,
        out_shape=[jax.ShapeDtypeStruct(shape, F32) for shape in shapes]
        + [jax.ShapeDtypeStruct(shape, BF16) for shape in shapes],
        in_specs=[pl.BlockSpec(memory_space=pltpu.HBM)] * 6,
        out_specs=[pl.BlockSpec(memory_space=pltpu.VMEM)] * 6,
        scratch_shapes=scratch,
        compiler_params=pltpu.CompilerParams(
            collective_id=0, has_side_effects=True, vmem_limit_bytes=32 * 1024 * 1024
        ),
        name="muon",
    )(
        *[
            pltpu.with_memory_space_constraint(value, pltpu.HBM)
            for value in (
                grad_wide[0, 0],
                grad_down[0, 0].T,
                grad_embed[0].T,
                mom_wide[0],
                mom_down[0].T,
                mom_embed.T,
            )
        ]
    )
    outs = pl.pallas_call(
        store_kernel,
        out_shape=[jax.ShapeDtypeStruct(o.shape, o.dtype) for o in outs],
        in_specs=[pl.BlockSpec(memory_space=pl.ANY)] * 6,
        out_specs=[pl.BlockSpec(memory_space=pltpu.HBM)] * 6,
        scratch_shapes=[dma((6,))],
        compiler_params=pltpu.CompilerParams(vmem_limit_bytes=1024 * 1024),
        name="store",
    )(*outs)
    new_wide, new_down, new_embed, upd_wide, upd_down, upd_embed = outs
    return (
        new_wide[None],
        new_down.T[None],
        new_embed.T,
        upd_wide[None],
        upd_down.T[None],
        upd_embed.T,
    )


def solution(mesh):
    return jax.shard_map(
        per_device,
        mesh=mesh,
        in_specs=(
            P("rep", None, "shard", None),
            P("rep", None, None, "shard"),
            P("rep", None, "shard"),
            P(None, "shard", None),
            P(None, None, "shard"),
            P(None, "shard"),
        ),
        out_specs=(
            P(None, "shard", None),
            P(None, None, "shard"),
            P(None, "shard"),
        )
        * 2,
        check_vma=False,
    )
```

```python
import math

import jax
import jax.numpy as jnp
from jax import lax
from jax.experimental import pallas as pl
from jax.experimental.pallas import tpu as pltpu
from jax.sharding import PartitionSpec as P

D = 384
COEF_A = 3.4445
COEF_B = -4.775
COEF_C = 2.0315
MOMENTUM = 0.95
EPSILON = 1e-07
NS_ITERS = 5

REP = 16
SHARD = 16
CHIPS_Z = 8
ROWS = D // SHARD
LANES = 128
WIDE, DOWN, EMBED = 5376, 1536, 1001
TILES = 62
SLOT = 5
GROUPS = 6
CHUNKS = ((4, 1), (0, 1), (1, 1), (2, 1), (3, 1))
FAR = ((2, 2), (1, 2), (3, 2), (0, 2), (2, 1), (2, 3), (1, 1), (3, 3), (1, 3), (3, 1), (0, 1), (0, 3), (2, 0), (1, 0), (3, 0))
STARTS = (0, 3, 6, 9, 12, 16, 20, 54, 24, 29, 34, 38, 42, 46, 50, 58)
WIDTHS = (3, 3, 3, 3, 4, 4, 4, 4, 5, 5, 4, 4, 4, 4, 4, 4)
FACTORS = (1152, 1152, 1152, 384, 1536, 1536, 1536, 1001) + (2304,) * 4 + (1536,) * 3 + (1001,)
MESH = pl.DeviceIdType.MESH
BF16 = jnp.bfloat16
F32 = jnp.float32


def tile_of(wide, down, embed, tile):
    if tile < 42:
        return wide[:, tile * LANES : (tile + 1) * LANES]
    if tile < 54:
        return down[:, (tile - 42) * LANES : (tile - 41) * LANES]
    first = (tile - 54) * LANES
    if tile < 61:
        return embed[:, first : first + LANES]
    part = embed[:, first:EMBED]
    return jnp.concatenate([part, jnp.zeros((ROWS, first + LANES - EMBED), part.dtype)], axis=1)


def put_tile(wide, down, embed, tile, value):
    if tile < 42:
        wide[:, tile * LANES : (tile + 1) * LANES] = value
    elif tile < 54:
        down[:, (tile - 42) * LANES : (tile - 41) * LANES] = value
    else:
        first = (tile - 54) * LANES
        width = min(LANES, EMBED - first)
        embed[:, first : first + width] = value[:, :width]


def split(value):
    high = value.astype(BF16)
    return high, (value - high.astype(F32)).astype(BF16)


def dot(left, right):
    return jnp.dot(left, right, preferred_element_type=F32)


def kernel(
    gw, gd, ge, mw, md, me_,
    ow, od, oe, uw, ud, ue,
    vgw, vgd, vge, vmw, vmd, vme,
    send, recv, slots_m, x, gall, part, group, tri, upd,
    load_sem, rs_s, rs_r, ga_s, ga_r, gae_s, gae_r, z_s, z_r, f_s, f_r, gr_s, gr_r, az_s, az_r, af_s, af_r,
    up_s, up_r, upe_s, upe_r,
):
    r = lax.axis_index("rep")
    s = lax.axis_index("shard")
    z = s // 2
    c = s % 2
    partner = z * 2 + (1 - c)
    five = r // 2 == 4

    def rep_to(d):
        return (r // 4 + FAR[d - 1][1]) % 4 * 4 + (r + FAR[d - 1][0]) % 4

    barrier = pltpu.get_barrier_semaphore()

    def greet(device):
        pl.semaphore_signal(barrier, inc=1, device_id=device, device_id_type=MESH)

    for d in (4, 3, 5, 2, 6, 1, 7):
        greet((r, (z + d) % CHIPS_Z * 2 + c))
    for d in range(1, REP):
        greet((rep_to(d), s))
    greet((r, partner))

    loads = [
        pltpu.make_async_copy(a, b, load_sem.at[i])
        for i, (a, b) in enumerate(((gw, vgw), (gd, vgd), (ge, vge), (mw, vmw), (md, vmd), (me_, vme)))
    ]
    for load in loads:
        load.start()

    for load in loads[:3]:
        load.wait()
    for k in range(REP):
        for t in range(SLOT):
            if t < WIDTHS[k]:
                send[k, t] = tile_of(vgw, vgd, vge, STARTS[k] + t).astype(BF16)
            else:
                send[k, t] = jnp.zeros((ROWS, LANES), BF16)

    pl.semaphore_wait(barrier, REP - 1 + CHIPS_Z - 1 + 1)

    def rcopy(src, dst, ss, rs, device):
        return pltpu.make_async_remote_copy(
            src_ref=src, dst_ref=dst, send_sem=ss, recv_sem=rs, device_id=device, device_id_type=MESH
        )

    def settle(ref, sem):
        rcopy(ref, ref, sem, sem, (r, partner)).wait_recv()

    def when_held(chunk, condition, body):
        if CHUNKS[chunk][0] == SLOT - 1:
            pl.when(condition)(body)
        else:
            body()

    def tiles(chunk):
        return pl.ds(*CHUNKS[chunk])

    def rs(d, chunk):
        to = rep_to(d)
        return rcopy(send.at[to, tiles(chunk)], recv.at[d, tiles(chunk)], rs_s.at[CHUNKS[chunk][0] // 4], rs_r.at[chunk], (to, s))

    for chunk in range(len(CHUNKS)):
        for d in range(1, REP):
            when_held(chunk, rep_to(d) // 2 == 4, rs(d, chunk).start)

    for load in loads[3:]:
        load.wait()
    for k in range(REP):
        for t in range(SLOT):
            if t < WIDTHS[k]:
                slots_m[k, t] = tile_of(vmw, vmd, vme, STARTS[k] + t)
            else:
                slots_m[k, t] = jnp.zeros((ROWS, LANES), F32)

    @pl.when(jnp.logical_not(five))
    def _():
        x[SLOT - 1] = jnp.zeros((D, LANES), BF16)

    def rows_of(shard):
        return pl.ds(pl.multiple_of(shard * ROWS, 8), ROWS)

    my_rows = rows_of(s)

    def reduce_tile(t):
        total = send[r, t].astype(F32)
        for d in range(1, REP):
            total = total + recv[d, t].astype(F32)
        momentum = MOMENTUM * slots_m[r, t] + total
        gall[r, t] = total.astype(BF16)
        x[t, my_rows, :] = (total + MOMENTUM * momentum).astype(BF16)

    def z_from(d):
        return (z - d + CHIPS_Z) % CHIPS_Z * 2 + c

    def z_to(d):
        return (z + d) % CHIPS_Z * 2 + c

    def zc(d, chunk):
        ref = x.at[tiles(chunk), my_rows, :]
        return rcopy(ref, ref, z_s.at[CHUNKS[chunk][0] // 4], z_r.at[chunk], (r, z_to(d)))

    def fc(d, chunk):
        ref = x.at[tiles(chunk), rows_of(z_from(d)), :]
        return rcopy(ref, ref, f_s.at[CHUNKS[chunk][0] // 4], f_r.at[chunk], (r, partner))

    far = (4, 3, 5, 2, 6, 1, 7)

    def scatter(chunk):
        settle(recv.at[pl.ds(1, REP - 1), tiles(chunk)], rs_r.at[chunk])
        start, size = CHUNKS[chunk]
        for t in range(start, start + size):
            reduce_tile(t)
        for d in far:
            zc(d, chunk).start()

    def forward(chunk):
        settle(x.at[tiles(chunk), pl.ds(0, (CHIPS_Z - 1) * ROWS), :], z_r.at[chunk])
        for d in range(CHIPS_Z):
            fc(d, chunk).start()

    for chunk in range(len(CHUNKS)):
        when_held(chunk, five, lambda chunk=chunk: scatter(chunk))

    def spread(buffer, send_sem, recv_sem, extra_send, extra_recv):
        for d in range(1, REP):
            ref = buffer.at[r, 0:4]
            rcopy(ref, ref, send_sem, recv_sem, (rep_to(d), s)).start()

        @pl.when(five)
        def _():
            for d in range(1, REP):
                ref = buffer.at[r, 4:5]
                rcopy(ref, ref, extra_send, extra_recv, (rep_to(d), s)).start()

    def spread_arrived(buffer, recv_sem, extra_recv):
        settle(buffer.at[0 : REP - 1, 0:4], recv_sem)

        @pl.when(five)
        def _():
            settle(buffer.at[8:9, 4:5], extra_recv)

        @pl.when(jnp.logical_not(five))
        def _():
            settle(buffer.at[8:10, 4:5], extra_recv)

    def spread_sent(buffer, send_sem, extra_send):
        settle(buffer.at[0 : REP - 1, 0:4], send_sem)

        @pl.when(five)
        def _():
            settle(buffer.at[0 : REP - 1, 4:5], extra_send)

    spread(gall, ga_s, ga_r, gae_s, gae_r)

    for chunk in range(len(CHUNKS)):
        when_held(chunk, five, lambda chunk=chunk: forward(chunk))

    def whole(chunk):
        return x.at[tiles(chunk), pl.ds(0, CHIPS_Z * ROWS), :]

    for chunk in range(len(CHUNKS)):
        when_held(chunk, five, lambda chunk=chunk: settle(whole(chunk), f_r.at[chunk]))

    whole_x = jnp.concatenate([x[t] for t in range(SLOT)], axis=1)
    mine = []
    blocks = []
    for j in range(GROUPS):
        g = s * GROUPS + j
        block = g // 16
        row_block = jnp.where(block < 3, 0, jnp.where(block < 5, 1, 2))
        column_block = jnp.where(block < 3, block, jnp.where(block < 5, block - 2, 2))
        start = pl.multiple_of(row_block * LANES + g % 16 * 8, 8)
        mine.append(jnp.concatenate([x[t, pl.ds(start, 8), :] for t in range(SLOT)], axis=1))
        blocks.append(column_block)
    gram = lax.dot_general(
        jnp.concatenate(mine, axis=0), whole_x, (((1,), (1,)), ((), ())), preferred_element_type=F32
    )
    for j in range(GROUPS):
        rows = gram[8 * j : 8 * j + 8]
        part[8 * j : 8 * j + 8, :] = jnp.where(
            blocks[j] == 0,
            rows[:, :LANES],
            jnp.where(blocks[j] == 1, rows[:, LANES : 2 * LANES], rows[:, 2 * LANES :]),
        )

    first = jnp.where(r // 4 == 2, 8, r // 4 * 4)
    count = jnp.where(r // 4 == 2, 4, 3)
    embed = jnp.logical_or(r == 7, r == 15)
    count = jnp.where(embed, 2, jnp.where(r == 3, 1, count))

    def member(d):
        place = r - first + d
        inside = first + jnp.where(place >= count, place - count, place)
        return jnp.where(embed, (r + 8) % REP, inside)

    def gr(d):
        return rcopy(part, group.at[d], gr_s.at[d], gr_r.at[d], (member(d), s))

    for d in range(1, 4):

        @pl.when(d < count)
        def _():
            gr(d).start()

    def share(shard):
        return pl.ds(pl.multiple_of(shard * (8 * GROUPS), 8), 8 * GROUPS)

    my_share = share(s)
    tri[my_share, :] = part[...]
    for d in range(1, 4):

        @pl.when(d < count)
        def _():
            gr(d).wait_recv()
            tri[my_share, :] = tri[my_share, :] + group[d]

    def az(d):
        ref = tri.at[my_share, :]
        return rcopy(ref, ref, az_s, az_r.at[d], (r, z_to(d)))

    def af(d):
        ref = tri.at[share(z_from(d)), :]
        return rcopy(ref, ref, af_s, af_r, (r, partner))

    for d in far:
        az(d).start()
    af(0).start()

    spread_arrived(gall, ga_r, gae_r)
    for k in range(REP):
        for t in range(WIDTHS[k]):
            put_tile(ow, od, oe, STARTS[k] + t, MOMENTUM * slots_m[k, t] + gall[k, t].astype(F32))

    for d in far:
        az(d).wait_recv()
        af(d).start()
    settle(tri.at[pl.ds(0, 3 * LANES), :], af_r)

    b0, b1, b2, b3, b4, b5 = (tri[b * LANES : (b + 1) * LANES, :] for b in range(6))
    a = jnp.concatenate(
        [
            jnp.concatenate([b0, b1, b2], axis=1),
            jnp.concatenate([b1.T, b3, b4], axis=1),
            jnp.concatenate([b2.T, b4.T, b5], axis=1),
        ],
        axis=0,
    )
    row = lax.broadcasted_iota(jnp.int32, (LANES, LANES), 0)
    column = lax.broadcasted_iota(jnp.int32, (LANES, LANES), 1)
    diagonal = jnp.where(row == column, b0 + b3 + b5, 0.0)
    trace = jnp.sum(jnp.sum(diagonal, axis=0, keepdims=True), axis=1, keepdims=True)
    scale = 1.0 / (jnp.sqrt(trace) + EPSILON)
    a = a * scale * scale

    lane = lax.broadcasted_iota(jnp.int32, (D, LANES), 1)
    q = jnp.where(
        jnp.logical_and(lax.broadcasted_iota(jnp.int32, (D, LANES), 0) - s * ROWS == lane, lane < ROWS), 1.0, 0.0
    )

    def product(value, right):
        high = value.astype(BF16)
        return dot(high if right.shape[0] == D else jnp.concatenate([high, high], axis=1), right)

    def stacked(value, fine):
        high, low = split(value)
        return jnp.concatenate([high, low], axis=0) if fine else high

    for step in range(NS_ITERS):
        if step < NS_ITERS - 1:
            fine = step >= 2
            right = jnp.concatenate([stacked(a, fine), stacked(q, fine)], axis=1)
            out = product(a, right)
            a2, qa = out[:, :D], out[:, D:]
            out = product(a2, right)
            a3, qa2 = out[:, :D], out[:, D:]
            b = COEF_A * a + COEF_B * a2 + COEF_C * a3
            a = COEF_A * b + product(COEF_B * a + COEF_C * a2, stacked(b, fine))
        else:
            qh, ql = split(q)
            left = jnp.concatenate(split(a), axis=1)

            def times(high, low):
                both = jnp.concatenate([high, low], axis=1)
                out = dot(left, jnp.concatenate([both, both], axis=0))
                return out[:, :LANES] + out[:, LANES:]

            qa = times(qh, ql)
            qa2 = times(*split(qa))
        q = COEF_A * q + COEF_B * qa + COEF_C * qa2

    factor = jnp.float32(0.0)
    for k in range(REP):
        factor = factor + jnp.where(r == k, jnp.float32(math.sqrt(max(D, FACTORS[k]))), jnp.float32(0.0))
    whole_x = jnp.concatenate([x[t] for t in range(SLOT)], axis=1)
    result = (dot(q.T[:ROWS].astype(BF16), whole_x) * (scale * factor)).astype(BF16)
    for t in range(SLOT):
        upd[r, t] = result[:, t * LANES : (t + 1) * LANES]

    spread(upd, up_s, up_r, upe_s, upe_r)

    spread_sent(gall, ga_s, gae_s)
    settle(send.at[0 : REP - 1, 0:4], rs_s.at[0])
    settle(x.at[0:4, pl.ds(0, (CHIPS_Z - 1) * ROWS), :], z_s.at[0])
    settle(x.at[0:4, pl.ds(0, CHIPS_Z * ROWS), :], f_s.at[0])

    @pl.when(five)
    def _():
        settle(send.at[0:1, 4:5], rs_s.at[1])
        settle(x.at[4:5, pl.ds(0, (CHIPS_Z - 1) * ROWS), :], z_s.at[1])
        settle(x.at[4:5, pl.ds(0, CHIPS_Z * ROWS), :], f_s.at[1])

    @pl.when(jnp.logical_not(five))
    def _():
        settle(send.at[0:2, 4:5], rs_s.at[1])

    settle(tri.at[pl.ds(0, (CHIPS_Z - 1) * 8 * GROUPS), :], az_s)
    settle(tri.at[pl.ds(0, 3 * LANES), :], af_s)
    for d in range(1, 4):

        @pl.when(d < count)
        def _():
            gr(d).wait_send()

    spread_arrived(upd, up_r, upe_r)
    for k in range(REP):
        for t in range(WIDTHS[k]):
            put_tile(uw, ud, ue, STARTS[k] + t, upd[k, t])
    spread_sent(upd, up_s, upe_s)


def store_kernel(*refs):
    sources, targets, sem = refs[:6], refs[6:12], refs[12]
    copies = [pltpu.make_async_copy(a, b, sem.at[i]) for i, (a, b) in enumerate(zip(sources, targets))]
    for copy in copies:
        copy.start()
    for copy in copies:
        copy.wait()


def per_device(grad_wide, grad_down, grad_embed, mom_wide, mom_down, mom_embed):
    shapes = [(ROWS, WIDE), (ROWS, DOWN), (ROWS, EMBED)]
    dma = pltpu.SemaphoreType.DMA
    scratch = (
        [pltpu.VMEM(shape, F32) for shape in shapes] * 2
        + [
            pltpu.VMEM((REP, SLOT, ROWS, LANES), BF16),
            pltpu.VMEM((REP, SLOT, ROWS, LANES), BF16),
            pltpu.VMEM((REP, SLOT, ROWS, LANES), F32),
            pltpu.VMEM((SLOT, D, LANES), BF16),
            pltpu.VMEM((REP, SLOT, ROWS, LANES), BF16),
            pltpu.VMEM((8 * GROUPS, LANES), F32),
            pltpu.VMEM((4, 8 * GROUPS, LANES), F32),
            pltpu.VMEM((6 * LANES, LANES), F32),
            pltpu.VMEM((REP, SLOT, ROWS, LANES), BF16),
        ]
        + [dma((6,))]
        + [dma((2,)), dma((len(CHUNKS),))]
        + [dma(())] * 4
        + [dma((2,)), dma((len(CHUNKS),))] * 2
        + [dma((4,))] * 2
        + [dma(()), dma((CHIPS_Z,)), dma(()), dma(())]
        + [dma(())] * 4
    )
    outs = pl.pallas_call(
        kernel,
        out_shape=[jax.ShapeDtypeStruct(shape, F32) for shape in shapes]
        + [jax.ShapeDtypeStruct(shape, BF16) for shape in shapes],
        in_specs=[pl.BlockSpec(memory_space=pltpu.HBM)] * 6,
        out_specs=[pl.BlockSpec(memory_space=pltpu.VMEM)] * 6,
        scratch_shapes=scratch,
        compiler_params=pltpu.CompilerParams(
            collective_id=0, has_side_effects=True, vmem_limit_bytes=32 * 1024 * 1024
        ),
        name="muon",
    )(
        *[
            pltpu.with_memory_space_constraint(value, pltpu.HBM)
            for value in (
                grad_wide[0, 0],
                grad_down[0, 0].T,
                grad_embed[0].T,
                mom_wide[0],
                mom_down[0].T,
                mom_embed.T,
            )
        ]
    )
    outs = pl.pallas_call(
        store_kernel,
        out_shape=[jax.ShapeDtypeStruct(o.shape, o.dtype) for o in outs],
        in_specs=[pl.BlockSpec(memory_space=pl.ANY)] * 6,
        out_specs=[pl.BlockSpec(memory_space=pltpu.HBM)] * 6,
        scratch_shapes=[dma((6,))],
        compiler_params=pltpu.CompilerParams(vmem_limit_bytes=1024 * 1024),
        name="store",
    )(*outs)
    new_wide, new_down, new_embed, upd_wide, upd_down, upd_embed = outs
    return (
        new_wide[None],
        new_down.T[None],
        new_embed.T,
        upd_wide[None],
        upd_down.T[None],
        upd_embed.T,
    )


def solution(mesh):
    return jax.shard_map(
        per_device,
        mesh=mesh,
        in_specs=(
            P("rep", None, "shard", None),
            P("rep", None, None, "shard"),
            P("rep", None, "shard"),
            P(None, "shard", None),
            P(None, None, "shard"),
            P(None, "shard"),
        ),
        out_specs=(
            P(None, "shard", None),
            P(None, None, "shard"),
            P(None, "shard"),
        )
        * 2,
        check_vma=False,
    )
```

```python
import math

import jax
import jax.numpy as jnp
from jax import lax
from jax.experimental import pallas as pl
from jax.experimental.pallas import tpu as pltpu
from jax.sharding import PartitionSpec as P

D = 384
COEF_A = 3.4445
COEF_B = -4.775
COEF_C = 2.0315
MOMENTUM = 0.95
EPSILON = 1e-07
NS_ITERS = 5

REP = 16
SHARD = 16
CHIPS_Z = 8
ROWS = D // SHARD
LANES = 128
WIDE, DOWN, EMBED = 5376, 1536, 1001
TILES = 62
SLOT = 5
GROUPS = 6
CHUNKS = ((4, 1), (0, 1), (1, 1), (2, 1), (3, 1))
FAR = ((2, 2), (1, 2), (3, 2), (0, 2), (2, 1), (2, 3), (1, 1), (3, 3), (1, 3), (3, 1), (0, 1), (0, 3), (2, 0), (1, 0), (3, 0))
STARTS = (0, 3, 6, 9, 12, 16, 20, 54, 24, 29, 34, 38, 42, 46, 50, 58)
WIDTHS = (3, 3, 3, 3, 4, 4, 4, 4, 5, 5, 4, 4, 4, 4, 4, 4)
FACTORS = (1152, 1152, 1152, 384, 1536, 1536, 1536, 1001) + (2304,) * 4 + (1536,) * 3 + (1001,)
MESH = pl.DeviceIdType.MESH
BF16 = jnp.bfloat16
F32 = jnp.float32


def tile_of(wide, down, embed, tile):
    if tile < 42:
        return wide[:, tile * LANES : (tile + 1) * LANES]
    if tile < 54:
        return down[:, (tile - 42) * LANES : (tile - 41) * LANES]
    first = (tile - 54) * LANES
    if tile < 61:
        return embed[:, first : first + LANES]
    part = embed[:, first:EMBED]
    return jnp.concatenate([part, jnp.zeros((ROWS, first + LANES - EMBED), part.dtype)], axis=1)


def put_tile(wide, down, embed, tile, value):
    if tile < 42:
        wide[:, tile * LANES : (tile + 1) * LANES] = value
    elif tile < 54:
        down[:, (tile - 42) * LANES : (tile - 41) * LANES] = value
    else:
        first = (tile - 54) * LANES
        width = min(LANES, EMBED - first)
        embed[:, first : first + width] = value[:, :width]


def split(value):
    high = value.astype(BF16)
    return high, (value - high.astype(F32)).astype(BF16)


def dot(left, right):
    return jnp.dot(left, right, preferred_element_type=F32)


def kernel(
    gw, gd, ge, mw, md, me_,
    ow, od, oe, uw, ud, ue,
    vgw, vgd, vge, vmw, vmd, vme,
    send, recv, slots_m, x, gall, part, group, tri, upd,
    load_sem, rs_s, rs_r, ga_s, ga_r, gae_s, gae_r, z_s, z_r, f_s, f_r, gr_s, gr_r, az_s, az_r, af_s, af_r,
    up_s, up_r, upe_s, upe_r,
):
    r = lax.axis_index("rep")
    s = lax.axis_index("shard")
    z = s // 2
    c = s % 2
    partner = z * 2 + (1 - c)
    five = r // 2 == 4

    def rep_to(d):
        return (r // 4 + FAR[d - 1][1]) % 4 * 4 + (r + FAR[d - 1][0]) % 4

    barrier = pltpu.get_barrier_semaphore()

    def greet(device):
        pl.semaphore_signal(barrier, inc=1, device_id=device, device_id_type=MESH)

    for d in (4, 3, 5, 2, 6, 1, 7):
        greet((r, (z + d) % CHIPS_Z * 2 + c))
    for d in range(1, REP):
        greet((rep_to(d), s))
    greet((r, partner))

    loads = [
        pltpu.make_async_copy(a, b, load_sem.at[i])
        for i, (a, b) in enumerate(((gw, vgw), (gd, vgd), (ge, vge), (mw, vmw), (md, vmd), (me_, vme)))
    ]
    for load in loads:
        load.start()

    for load in loads[:3]:
        load.wait()
    for k in range(REP):
        for t in range(SLOT):
            if t < WIDTHS[k]:
                send[k, t] = tile_of(vgw, vgd, vge, STARTS[k] + t).astype(BF16)
            else:
                send[k, t] = jnp.zeros((ROWS, LANES), BF16)

    pl.semaphore_wait(barrier, REP - 1 + CHIPS_Z - 1 + 1)

    def rcopy(src, dst, ss, rs, device):
        return pltpu.make_async_remote_copy(
            src_ref=src, dst_ref=dst, send_sem=ss, recv_sem=rs, device_id=device, device_id_type=MESH
        )

    def settle(ref, sem):
        rcopy(ref, ref, sem, sem, (r, partner)).wait_recv()

    def when_held(chunk, condition, body):
        if CHUNKS[chunk][0] == SLOT - 1:
            pl.when(condition)(body)
        else:
            body()

    def tiles(chunk):
        return pl.ds(*CHUNKS[chunk])

    def rs(d, chunk):
        to = rep_to(d)
        return rcopy(send.at[to, tiles(chunk)], recv.at[d, tiles(chunk)], rs_s.at[CHUNKS[chunk][0] // 4], rs_r.at[chunk], (to, s))

    for chunk in range(len(CHUNKS)):
        for d in range(1, REP):
            when_held(chunk, rep_to(d) // 2 == 4, rs(d, chunk).start)

    for load in loads[3:]:
        load.wait()
    for k in range(REP):
        for t in range(SLOT):
            if t < WIDTHS[k]:
                slots_m[k, t] = tile_of(vmw, vmd, vme, STARTS[k] + t)
            else:
                slots_m[k, t] = jnp.zeros((ROWS, LANES), F32)

    @pl.when(jnp.logical_not(five))
    def _():
        x[SLOT - 1] = jnp.zeros((D, LANES), BF16)

    def rows_of(shard):
        return pl.ds(pl.multiple_of(shard * ROWS, 8), ROWS)

    my_rows = rows_of(s)

    def reduce_tile(t):
        total = send[r, t].astype(F32)
        for d in range(1, REP):
            total = total + recv[d, t].astype(F32)
        momentum = MOMENTUM * slots_m[r, t] + total
        gall[r, t] = total.astype(BF16)
        x[t, my_rows, :] = (total + MOMENTUM * momentum).astype(BF16)

    def z_from(d):
        return (z - d + CHIPS_Z) % CHIPS_Z * 2 + c

    def z_to(d):
        return (z + d) % CHIPS_Z * 2 + c

    def zc(d, chunk):
        ref = x.at[tiles(chunk), my_rows, :]
        return rcopy(ref, ref, z_s.at[CHUNKS[chunk][0] // 4], z_r.at[chunk], (r, z_to(d)))

    def fc(d, chunk):
        ref = x.at[tiles(chunk), rows_of(z_from(d)), :]
        return rcopy(ref, ref, f_s.at[CHUNKS[chunk][0] // 4], f_r.at[chunk], (r, partner))

    far = (4, 3, 5, 2, 6, 1, 7)

    def scatter(chunk):
        settle(recv.at[pl.ds(1, REP - 1), tiles(chunk)], rs_r.at[chunk])
        start, size = CHUNKS[chunk]
        for t in range(start, start + size):
            reduce_tile(t)
        for d in far:
            zc(d, chunk).start()

    def forward(chunk):
        settle(x.at[tiles(chunk), pl.ds(0, (CHIPS_Z - 1) * ROWS), :], z_r.at[chunk])
        for d in range(CHIPS_Z):
            fc(d, chunk).start()

    for chunk in range(len(CHUNKS)):
        when_held(chunk, five, lambda chunk=chunk: scatter(chunk))

    def spread(buffer, send_sem, recv_sem, extra_send, extra_recv):
        def main(d):
            ref = buffer.at[r, 0:4]
            rcopy(ref, ref, send_sem, recv_sem, (rep_to(d), s)).start()

        @pl.when(five)
        def _():
            for d in range(1, REP):
                ref = buffer.at[r, 4:5]
                rcopy(ref, ref, extra_send, extra_recv, (rep_to(d), s)).start()
                main(d)

        @pl.when(jnp.logical_not(five))
        def _():
            for d in range(1, REP):
                main(d)

    def spread_arrived(buffer, recv_sem, extra_recv):
        settle(buffer.at[0 : REP - 1, 0:4], recv_sem)

        @pl.when(five)
        def _():
            settle(buffer.at[8:9, 4:5], extra_recv)

        @pl.when(jnp.logical_not(five))
        def _():
            settle(buffer.at[8:10, 4:5], extra_recv)

    def spread_sent(buffer, send_sem, extra_send):
        settle(buffer.at[0 : REP - 1, 0:4], send_sem)

        @pl.when(five)
        def _():
            settle(buffer.at[0 : REP - 1, 4:5], extra_send)

    spread(gall, ga_s, ga_r, gae_s, gae_r)

    for chunk in range(len(CHUNKS)):
        when_held(chunk, five, lambda chunk=chunk: forward(chunk))

    def whole(chunk):
        return x.at[tiles(chunk), pl.ds(0, CHIPS_Z * ROWS), :]

    for chunk in range(len(CHUNKS)):
        when_held(chunk, five, lambda chunk=chunk: settle(whole(chunk), f_r.at[chunk]))

    whole_x = jnp.concatenate([x[t] for t in range(SLOT)], axis=1)
    mine = []
    blocks = []
    for j in range(GROUPS):
        g = s * GROUPS + j
        block = g // 16
        row_block = jnp.where(block < 3, 0, jnp.where(block < 5, 1, 2))
        column_block = jnp.where(block < 3, block, jnp.where(block < 5, block - 2, 2))
        start = pl.multiple_of(row_block * LANES + g % 16 * 8, 8)
        mine.append(jnp.concatenate([x[t, pl.ds(start, 8), :] for t in range(SLOT)], axis=1))
        blocks.append(column_block)
    gram = lax.dot_general(
        jnp.concatenate(mine, axis=0), whole_x, (((1,), (1,)), ((), ())), preferred_element_type=F32
    )
    for j in range(GROUPS):
        rows = gram[8 * j : 8 * j + 8]
        part[8 * j : 8 * j + 8, :] = jnp.where(
            blocks[j] == 0,
            rows[:, :LANES],
            jnp.where(blocks[j] == 1, rows[:, LANES : 2 * LANES], rows[:, 2 * LANES :]),
        )

    first = jnp.where(r // 4 == 2, 8, r // 4 * 4)
    count = jnp.where(r // 4 == 2, 4, 3)
    embed = jnp.logical_or(r == 7, r == 15)
    count = jnp.where(embed, 2, jnp.where(r == 3, 1, count))

    def member(d):
        place = r - first + d
        inside = first + jnp.where(place >= count, place - count, place)
        return jnp.where(embed, (r + 8) % REP, inside)

    def gr(d):
        return rcopy(part, group.at[d], gr_s.at[d], gr_r.at[d], (member(d), s))

    for d in range(1, 4):

        @pl.when(d < count)
        def _():
            gr(d).start()

    def share(shard):
        return pl.ds(pl.multiple_of(shard * (8 * GROUPS), 8), 8 * GROUPS)

    my_share = share(s)
    tri[my_share, :] = part[...]
    for d in range(1, 4):

        @pl.when(d < count)
        def _():
            gr(d).wait_recv()
            tri[my_share, :] = tri[my_share, :] + group[d]

    def az(d):
        ref = tri.at[my_share, :]
        return rcopy(ref, ref, az_s, az_r.at[d], (r, z_to(d)))

    def af(d):
        ref = tri.at[share(z_from(d)), :]
        return rcopy(ref, ref, af_s, af_r, (r, partner))

    for d in far:
        az(d).start()
    af(0).start()

    spread_arrived(gall, ga_r, gae_r)
    for k in range(REP):
        for t in range(WIDTHS[k]):
            put_tile(ow, od, oe, STARTS[k] + t, MOMENTUM * slots_m[k, t] + gall[k, t].astype(F32))

    for d in far:
        az(d).wait_recv()
        af(d).start()
    settle(tri.at[pl.ds(0, 3 * LANES), :], af_r)

    b0, b1, b2, b3, b4, b5 = (tri[b * LANES : (b + 1) * LANES, :] for b in range(6))
    a = jnp.concatenate(
        [
            jnp.concatenate([b0, b1, b2], axis=1),
            jnp.concatenate([b1.T, b3, b4], axis=1),
            jnp.concatenate([b2.T, b4.T, b5], axis=1),
        ],
        axis=0,
    )
    row = lax.broadcasted_iota(jnp.int32, (LANES, LANES), 0)
    column = lax.broadcasted_iota(jnp.int32, (LANES, LANES), 1)
    diagonal = jnp.where(row == column, b0 + b3 + b5, 0.0)
    trace = jnp.sum(jnp.sum(diagonal, axis=0, keepdims=True), axis=1, keepdims=True)
    scale = 1.0 / (jnp.sqrt(trace) + EPSILON)
    a = a * scale * scale

    lane = lax.broadcasted_iota(jnp.int32, (D, LANES), 1)
    q = jnp.where(
        jnp.logical_and(lax.broadcasted_iota(jnp.int32, (D, LANES), 0) - s * ROWS == lane, lane < ROWS), 1.0, 0.0
    )

    def product(value, right):
        high = value.astype(BF16)
        return dot(high if right.shape[0] == D else jnp.concatenate([high, high], axis=1), right)

    def stacked(value, fine):
        high, low = split(value)
        return jnp.concatenate([high, low], axis=0) if fine else high

    for step in range(NS_ITERS):
        if step < NS_ITERS - 1:
            fine = step >= 2
            right = jnp.concatenate([stacked(a, fine), stacked(q, fine)], axis=1)
            out = product(a, right)
            a2, qa = out[:, :D], out[:, D:]
            out = product(a2, right)
            a3, qa2 = out[:, :D], out[:, D:]
            b = COEF_A * a + COEF_B * a2 + COEF_C * a3
            a = COEF_A * b + product(COEF_B * a + COEF_C * a2, stacked(b, fine))
        else:
            qh, ql = split(q)
            left = jnp.concatenate(split(a), axis=1)

            def times(high, low):
                both = jnp.concatenate([high, low], axis=1)
                out = dot(left, jnp.concatenate([both, both], axis=0))
                return out[:, :LANES] + out[:, LANES:]

            qa = times(qh, ql)
            qa2 = times(*split(qa))
        q = COEF_A * q + COEF_B * qa + COEF_C * qa2

    factor = jnp.float32(0.0)
    for k in range(REP):
        factor = factor + jnp.where(r == k, jnp.float32(math.sqrt(max(D, FACTORS[k]))), jnp.float32(0.0))
    whole_x = jnp.concatenate([x[t] for t in range(SLOT)], axis=1)
    result = (dot(q.T[:ROWS].astype(BF16), whole_x) * (scale * factor)).astype(BF16)
    for t in range(SLOT):
        upd[r, t] = result[:, t * LANES : (t + 1) * LANES]

    spread(upd, up_s, up_r, upe_s, upe_r)

    spread_sent(gall, ga_s, gae_s)
    settle(send.at[0 : REP - 1, 0:4], rs_s.at[0])
    settle(x.at[0:4, pl.ds(0, (CHIPS_Z - 1) * ROWS), :], z_s.at[0])
    settle(x.at[0:4, pl.ds(0, CHIPS_Z * ROWS), :], f_s.at[0])

    @pl.when(five)
    def _():
        settle(send.at[0:1, 4:5], rs_s.at[1])
        settle(x.at[4:5, pl.ds(0, (CHIPS_Z - 1) * ROWS), :], z_s.at[1])
        settle(x.at[4:5, pl.ds(0, CHIPS_Z * ROWS), :], f_s.at[1])

    @pl.when(jnp.logical_not(five))
    def _():
        settle(send.at[0:2, 4:5], rs_s.at[1])

    settle(tri.at[pl.ds(0, (CHIPS_Z - 1) * 8 * GROUPS), :], az_s)
    settle(tri.at[pl.ds(0, 3 * LANES), :], af_s)
    for d in range(1, 4):

        @pl.when(d < count)
        def _():
            gr(d).wait_send()

    spread_arrived(upd, up_r, upe_r)
    for k in range(REP):
        for t in range(WIDTHS[k]):
            put_tile(uw, ud, ue, STARTS[k] + t, upd[k, t])
    spread_sent(upd, up_s, upe_s)


def store_kernel(*refs):
    sources, targets, sem = refs[:6], refs[6:12], refs[12]
    copies = [pltpu.make_async_copy(a, b, sem.at[i]) for i, (a, b) in enumerate(zip(sources, targets))]
    for copy in copies:
        copy.start()
    for copy in copies:
        copy.wait()


def per_device(grad_wide, grad_down, grad_embed, mom_wide, mom_down, mom_embed):
    shapes = [(ROWS, WIDE), (ROWS, DOWN), (ROWS, EMBED)]
    dma = pltpu.SemaphoreType.DMA
    scratch = (
        [pltpu.VMEM(shape, F32) for shape in shapes] * 2
        + [
            pltpu.VMEM((REP, SLOT, ROWS, LANES), BF16),
            pltpu.VMEM((REP, SLOT, ROWS, LANES), BF16),
            pltpu.VMEM((REP, SLOT, ROWS, LANES), F32),
            pltpu.VMEM((SLOT, D, LANES), BF16),
            pltpu.VMEM((REP, SLOT, ROWS, LANES), BF16),
            pltpu.VMEM((8 * GROUPS, LANES), F32),
            pltpu.VMEM((4, 8 * GROUPS, LANES), F32),
            pltpu.VMEM((6 * LANES, LANES), F32),
            pltpu.VMEM((REP, SLOT, ROWS, LANES), BF16),
        ]
        + [dma((6,))]
        + [dma((2,)), dma((len(CHUNKS),))]
        + [dma(())] * 4
        + [dma((2,)), dma((len(CHUNKS),))] * 2
        + [dma((4,))] * 2
        + [dma(()), dma((CHIPS_Z,)), dma(()), dma(())]
        + [dma(())] * 4
    )
    outs = pl.pallas_call(
        kernel,
        out_shape=[jax.ShapeDtypeStruct(shape, F32) for shape in shapes]
        + [jax.ShapeDtypeStruct(shape, BF16) for shape in shapes],
        in_specs=[pl.BlockSpec(memory_space=pltpu.HBM)] * 6,
        out_specs=[pl.BlockSpec(memory_space=pltpu.VMEM)] * 6,
        scratch_shapes=scratch,
        compiler_params=pltpu.CompilerParams(
            collective_id=0, has_side_effects=True, vmem_limit_bytes=32 * 1024 * 1024
        ),
        name="muon",
    )(
        *[
            pltpu.with_memory_space_constraint(value, pltpu.HBM)
            for value in (
                grad_wide[0, 0],
                grad_down[0, 0].T,
                grad_embed[0].T,
                mom_wide[0],
                mom_down[0].T,
                mom_embed.T,
            )
        ]
    )
    outs = pl.pallas_call(
        store_kernel,
        out_shape=[jax.ShapeDtypeStruct(o.shape, o.dtype) for o in outs],
        in_specs=[pl.BlockSpec(memory_space=pl.ANY)] * 6,
        out_specs=[pl.BlockSpec(memory_space=pltpu.HBM)] * 6,
        scratch_shapes=[dma((6,))],
        compiler_params=pltpu.CompilerParams(vmem_limit_bytes=1024 * 1024),
        name="store",
    )(*outs)
    new_wide, new_down, new_embed, upd_wide, upd_down, upd_embed = outs
    return (
        new_wide[None],
        new_down.T[None],
        new_embed.T,
        upd_wide[None],
        upd_down.T[None],
        upd_embed.T,
    )


def solution(mesh):
    return jax.shard_map(
        per_device,
        mesh=mesh,
        in_specs=(
            P("rep", None, "shard", None),
            P("rep", None, None, "shard"),
            P("rep", None, "shard"),
            P(None, "shard", None),
            P(None, None, "shard"),
            P(None, "shard"),
        ),
        out_specs=(
            P(None, "shard", None),
            P(None, None, "shard"),
            P(None, "shard"),
        )
        * 2,
        check_vma=False,
    )
```
